256 devices in a mesh: dp: 4 (over x), vocab: 64 (over z, y, core).
Axes of the slice: x: 4, y: 4, z: 8, core: 2. Of those that a mesh axis runs over, the one named last changes fastest.
Arguments:
- hidden_t: bfloat16 [8192, 768], P(('dp', 'vocab')), may hold values from -6 to 6
- head: bfloat16 [8192, 81920], P('dp', 'vocab'), may hold values from -0.2 to 0.2
- teacher: bfloat16 [768, 81920], P('dp', 'vocab'), may hold values from -16 to 960
- labels: int32 [768], P('dp'), may hold values from 0 to 81919
- temps: float32 [4], replicated, may hold values from 1 to 4
- mix: float32 [2], replicated, may hold values from 0.3 to 1
Outputs:
- hidden_grad: float32 [8192, 768], P(('dp', 'vocab'))
- head_grad: bfloat16 [8192, 81920], P('dp', 'vocab')
The draws below stay inside these ranges and needn't reach their ends.
All inputs are finite; a program needn't handle non-finite values.
Results may differ from the reference program's by a relative error of at most 0.012.
Values may be sent and summed in bfloat16 or wider, within the bound.
A program may use at most 128 MiB of HBM per device.

```python
import math
import jax
import jax.numpy as jnp
import numpy as np
from jax import lax

D = 8192
NTEMP = 4
VOCAB = 81920
TOKENS = 768


def draw_head(key, part):
    own_key = jax.random.fold_in(key, 11)
    values = jnp.clip(jax.random.normal(own_key, (D, VOCAB)) * 0.033, -0.2, 0.2)
    return values.astype(jnp.bfloat16)


def draw_hidden_t(key, part):
    own_key = jax.random.fold_in(key, 13)
    values = jnp.clip(jax.random.normal(own_key, (D, TOKENS)), -6.0, 6.0)
    return values.astype(jnp.bfloat16)


def draw_teacher(key, part):
    first_key = jax.random.fold_in(key, 0)
    values = jnp.clip(jax.random.normal(first_key, (TOKENS, VOCAB)) * 3.0, -12.0, 12.0)
    return values.astype(jnp.bfloat16)


def touch_ends(result, key, low, top_value):
    longest = result.shape.index(max(result.shape))
    spots = []
    for shift in (0, 1):
        where = [jax.random.randint(jax.random.fold_in(key, axis), (), 0, length) for axis, length in enumerate(result.shape)]
        where[longest] = (where[longest] + shift) % result.shape[longest]
        spots.append(tuple(where))
    return result.at[spots[0]].set(low).at[spots[1]].set(top_value)


def skewed_wide(stream_key, shape, count, slope):
    portions = [min(1 << octave, count + 1 - (1 << octave)) * (1 << 20) // math.isqrt((1 << octave) ** slope) + 1 for octave in range((count + 1).bit_length()) if 1 << octave <= count]
    width = 1 + sum(portions) // (1 << 30)
    grid = np.cumsum(np.array([max(1, weight // width) for weight in portions]))
    pick = jax.random.randint(jax.random.fold_in(stream_key, 1), shape, 0, int(grid[len(portions) - 1]))
    start = jnp.left_shift(1, jnp.searchsorted(jnp.asarray(grid, jnp.int32), pick, side="right").astype(jnp.int32))
    standing = start - 1 + jax.random.randint(jax.random.fold_in(stream_key, 4), shape, 0, 1 << 30) % jnp.minimum(start, count + 1 - start)
    return jax.random.permutation(jax.random.fold_in(stream_key, 2), count)[standing].astype(jnp.int32)


def setup_inputs(seed: int = 0) -> dict:
    key_list = jax.random.split(jax.random.key(seed), 7)
    hidden_t = draw_hidden_t(jax.random.fold_in(key_list[6], 71), 0)
    head = draw_head(jax.random.fold_in(key_list[6], 71), 0)
    teacher = draw_teacher(jax.random.fold_in(key_list[6], 71), 0)
    labels = touch_ends(skewed_wide(key_list[3], (TOKENS,), VOCAB, 2), jax.random.fold_in(key_list[3], 3), 0, VOCAB - 1).astype(jnp.int32)
    temps = jnp.clip(jnp.exp(jax.random.uniform(key_list[4], (NTEMP,), jnp.float32, math.log(1.0), math.log(4.0))), 1.0, 4.0)
    mix = jnp.clip(jax.random.uniform(key_list[5], (2,), jnp.float32, 0.3, 1.0), 0.3, 1.0)
    return {"hidden_t": hidden_t, "head": head, "teacher": teacher, "labels": labels, "temps": temps, "mix": mix}


def tempered(values):
    highest = jnp.max(values, axis=1, keepdims=True)
    expo = jnp.exp(values - highest)
    return expo / jnp.sum(expo, axis=1, keepdims=True)


def reference(hidden_t, head, teacher, labels, temps, mix):
    logits = lax.dot_general(hidden_t, head, (((0,), (0,)), ((), ())), preferred_element_type=jnp.float32)
    target = teacher.astype(jnp.float32)
    columns = jnp.arange(logits.shape[1], dtype=jnp.int32)
    onehot = (columns[None, :] == labels[:, None]).astype(jnp.float32)
    logit_grad = mix[0] * (tempered(logits) - onehot)
    for index in range(NTEMP):
        heat = temps[index]
        logit_grad = logit_grad + mix[1] * heat * (tempered(logits / heat) - tempered(target / heat))
    logit_grad = logit_grad.astype(jnp.bfloat16)
    hidden_grad = lax.dot_general(head, logit_grad, (((1,), (1,)), ((), ())), preferred_element_type=jnp.float32)
    head_grad = jnp.dot(hidden_t, logit_grad, preferred_element_type=jnp.float32).astype(jnp.bfloat16)
    return hidden_grad, head_grad
```

```python
import jax
import jax.numpy as jnp
from jax import lax
from jax.sharding import PartitionSpec as P


def shards(hidden_t, head, teacher, labels, temps, mix):
    h_block = lax.all_gather(hidden_t, "vocab", axis=0, tiled=True)
    block_width = head.shape[1]
    logits = lax.psum_scatter(
        lax.dot_general(
            h_block, head, (((0,), (0,)), ((), ())), preferred_element_type=jnp.float32
        ),
        "dp",
        scatter_dimension=0,
        tiled=True,
    )
    target = teacher.astype(jnp.float32)
    inverse = 1.0 / temps
    heat_count = temps.shape[0]
    all_inverse = jnp.concatenate([jnp.ones((1,), jnp.float32), inverse])
    student_peak = jnp.max(logits, axis=1)
    teacher_peak = jnp.max(target, axis=1)
    parts = [student_peak, teacher_peak]
    for k in range(1 + heat_count):
        parts.append(jnp.sum(jnp.exp((logits - student_peak[:, None]) * all_inverse[k]), axis=1))
    for k in range(heat_count):
        parts.append(jnp.sum(jnp.exp((target - teacher_peak[:, None]) * inverse[k]), axis=1))
    gathered = lax.all_gather(jnp.stack(parts), "vocab", axis=0)
    top = jnp.max(gathered[:, :2], axis=0)
    gap = gathered[:, :2] - top[None]
    denominators = []
    for k in range(1 + heat_count):
        denominators.append(jnp.sum(gathered[:, 2 + k] * jnp.exp(gap[:, 0] * all_inverse[k]), axis=0))
    for k in range(heat_count):
        denominators.append(
            jnp.sum(gathered[:, 3 + heat_count + k] * jnp.exp(gap[:, 1] * inverse[k]), axis=0)
        )
    columns = jnp.arange(block_width, dtype=jnp.int32)[None, :] + lax.axis_index("vocab") * block_width
    s_off = logits - top[0][:, None]
    t_off = target - top[1][:, None]
    grad = jnp.exp(s_off) * (mix[0] / denominators[0])[:, None]
    grad = grad - jnp.where(columns == labels[:, None], mix[0], 0.0)
    for k in range(heat_count):
        w = mix[1] * temps[k]
        grad = grad + jnp.exp(s_off * inverse[k]) * (w / denominators[1 + k])[:, None]
        grad = grad - jnp.exp(t_off * inverse[k]) * (w / denominators[1 + heat_count + k])[:, None]
    grad = grad.astype(jnp.bfloat16)
    grad_all = lax.all_gather(grad, "dp", axis=0, tiled=True)
    hidden_grad = lax.psum_scatter(
        lax.dot_general(
            head, grad_all, (((1,), (1,)), ((), ())), preferred_element_type=jnp.float32
        ),
        "vocab",
        scatter_dimension=0,
        tiled=True,
    )
    head_grad = jnp.dot(h_block, grad_all, preferred_element_type=jnp.float32).astype(jnp.bfloat16)
    return (hidden_grad, head_grad)


def solution(mesh):
    placed = (P(("dp", "vocab"), None), P("dp", "vocab"), P("dp", "vocab"), P("dp"), P(), P())
    return jax.shard_map(
        shards,
        mesh=mesh,
        in_specs=placed,
        out_specs=(P(("dp", "vocab"), None), P("dp", "vocab")),
        check_vma=False,
    )
```

```python
import functools

import jax
import jax.numpy as jnp
from jax import lax
from jax.experimental import pallas as pl
from jax.experimental.pallas import tpu as pltpu
from jax.sharding import PartitionSpec as P

BF = jnp.bfloat16
F32 = jnp.float32
MESH = pl.DeviceIdType.MESH
NX, NZ, NY, NC = 4, 8, 4, 2
TOK, OWN, HALF = 768, 192, 96
COLS, CW, NCH = 1280, 256, 5
FEAT, LROWS, CH = 2048, 32, 384
NT = 4
ORDER = (0, -1, 1, -2, 2, -3, 3, 4)


def body(hid, head_hbm, teach_hbm, labels, temps, mix,
         hgrad, hdgrad,
         hb, hd, ht, part, ra1, rb1, ra2, rb2, ra3, rb3, logit, teach,
         wt, st, r1, r2, ct, coef, grads, hg, ps, pr, zs, zr, ysb, yrb,
         loc_sem, own_sem, ay_s, ay_r, az_s, az_r, ap_s, ap_r,
         rx_s, rx_r, s1_s, s1_r, s2_s, s2_r, gx_s, gx_r,
         pp_s, pp_r, zz_s, zz_r, yy_s, yy_r):
    x = lax.axis_index("dp")
    v = lax.axis_index("vocab")
    c = lax.rem(v, 2)
    y = lax.rem(v // 2, NY)
    z = v // (NY * NC)

    def vid(zz, yy, cc):
        return {"vocab": (zz * NY + yy) * NC + cc}

    def zrel(d):
        return lax.rem(z + (d + NZ), NZ)

    def yrel(d):
        return lax.rem(y + (d + NY), NY)

    def xrel(d):
        return lax.rem(x + (d + NX), NX)

    zup, zdn = vid(zrel(1), y, c), vid(zrel(-1), y, c)
    yup, ydn = vid(z, yrel(1), c), vid(z, yrel(-1), c)
    mate = vid(z, y, 1 - c)
    xup, xdn = {"dp": xrel(1)}, {"dp": xrel(-1)}
    slot = y * NC + c

    def group1(k):
        other = lax.rem(slot + k, 8)
        return vid(z, other // NC, lax.rem(other, NC))

    def group2(k):
        return vid(zrel(k), y, c)

    def rcopy(src, dst, ssem, rsem, dev):
        return pltpu.make_async_remote_copy(
            src_ref=src, dst_ref=dst, send_sem=ssem, recv_sem=rsem,
            device_id=dev, device_id_type=MESH)

    sent = []

    def send(src, dst, ssem, rsem, dev):
        cp = rcopy(src, dst, ssem, rsem, dev)
        cp.start()
        sent.append(cp)
        return cp

    own_copy = pltpu.make_async_copy(hid, hb.at[z, y, c], own_sem)
    own_copy.start()
    head_copies = []
    for j in range(NCH):
        cp = pltpu.make_async_copy(head_hbm.at[:, pl.ds(j * CW, CW)], hd.at[j], loc_sem.at[j])
        cp.start()
        head_copies.append(cp)
    teach_copy = pltpu.make_async_copy(teach_hbm, teach, loc_sem.at[NCH])
    teach_copy.start()

    bar = pltpu.get_barrier_semaphore()
    for k in range(1, 8):
        pl.semaphore_signal(bar, inc=1, device_id=group1(k), device_id_type=MESH)
        pl.semaphore_signal(bar, inc=1, device_id=group2(k), device_id_type=MESH)
    pl.semaphore_signal(bar, inc=1, device_id=xup, device_id_type=MESH)
    pl.semaphore_signal(bar, inc=1, device_id=xdn, device_id_type=MESH)
    pl.semaphore_wait(bar, 16)

    y0 = send(hid, hb.at[z, y, c], ay_s.at[0], ay_r.at[0], yup)
    y1 = send(hid, hb.at[z, y, c], ay_s.at[1], ay_r.at[1], ydn)
    own_copy.wait()
    lo, hi = pl.ds(0, CH), pl.ds(CH, CH)
    y0.wait_recv()
    fw = hb.at[z, yrel(-1), c, :, lo]
    y2 = send(fw, fw, ay_s.at[2], ay_r.at[2], yup)
    y1.wait_recv()
    fw = hb.at[z, yrel(1), c, :, hi]
    y3 = send(fw, fw, ay_s.at[3], ay_r.at[3], ydn)
    y2.wait_recv()
    y3.wait_recv()

    def zsend(d, step):
        up = hb.at[zrel(-d), :, c]
        dn = hb.at[zrel(d), :, c]
        if step < 4:
            return (send(up, up, az_s.at[2 * step - 2], az_r.at[2 * step - 2], zup),
                    send(dn, dn, az_s.at[2 * step - 1], az_r.at[2 * step - 1], zdn))
        up = hb.at[zrel(-d), :, c, :, lo]
        dn = hb.at[zrel(d), :, c, :, hi]
        return (send(up, up, az_s.at[6], az_r.at[6], zup),
                send(dn, dn, az_s.at[7], az_r.at[7], zdn))

    def give(i):
        b = hb.at[zrel(ORDER[i]), :, c]
        return send(b, b, ap_s.at[i], ap_r.at[i], mate)

    gives = [None] * 8
    flights = zsend(0, 1)
    gives[0] = give(0)

    inv = [1.0 / temps[k] for k in range(NT)]
    lane = lax.broadcasted_iota(jnp.int32, (32, 128), 1)
    zeros32 = jnp.zeros((32, 128), F32)

    teach_copy.wait()

    @pl.loop(0, OWN // 32)
    def _(i):
        rows = pl.ds(pl.multiple_of(i * 32, 32), 32)
        t = teach[rows, :].astype(F32)
        m = jnp.max(t, axis=1, keepdims=True)
        t = t - m
        w = jnp.where(lane == 8, m, zeros32)
        for k in range(NT):
            w = jnp.where(lane == 9 + k, jnp.sum(jnp.exp(t * inv[k]), axis=1, keepdims=True), w)
        wt[rows, :] = w

    wt[pl.ds(OWN, 64), :] = jnp.zeros((64, 128), F32)

    for cp in head_copies:
        cp.wait()

    def flip(i):
        blk = hb[zrel(ORDER[i])].reshape(256, TOK)
        ht[i] = blk.T

    def mm(i, j):
        rows = pl.ds(pl.multiple_of(zrel(ORDER[i]) * 256, 256), 256)
        return jnp.dot(ht[i], hd[j, rows, :], preferred_element_type=F32)

    def stage(ids):
        for i in ids:
            gives[i].wait_recv()
            flip(i)

        @pl.loop(0, NCH)
        def _(j):
            acc = mm(ids[0], j)
            for i in ids[1:]:
                acc = acc + mm(i, j)
            if ids[0] != 0:
                acc = acc + part[j]
            part[j] = acc

    done = [0]
    for d in range(1, 5):
        for f in flights:
            f.wait_recv()
        if d < 4:
            flights = zsend(d, d + 1)
            gives[2 * d - 1] = give(2 * d - 1)
            gives[2 * d] = give(2 * d)
        else:
            gives[7] = give(7)
        if d == 1:
            stage([0])
        else:
            stage([2 * d - 3, 2 * d - 2])

    gives[7].wait_recv()
    flip(7)

    def tokens(d, half):
        return pl.ds(pl.multiple_of(xrel(d) * OWN + half * HALF, HALF), HALF)

    def far(j):
        return (rcopy(part.at[j, tokens(2, 0)], ra1.at[j], rx_s.at[0, j], rx_r.at[0, j], xup),
                rcopy(part.at[j, tokens(2, 1)], rb1.at[j], rx_s.at[1, j], rx_r.at[1, j], xdn))

    def near(j):
        return (rcopy(part.at[j, tokens(1, 1)], rb2.at[j], rx_s.at[2, j], rx_r.at[2, j], xup),
                rcopy(part.at[j, tokens(-1, 0)], ra2.at[j], rx_s.at[3, j], rx_r.at[3, j], xdn))

    def relay(j):
        return (rcopy(ra1.at[j], ra3.at[j], rx_s.at[4, j], rx_r.at[4, j], xup),
                rcopy(rb1.at[j], rb3.at[j], rx_s.at[5, j], rx_r.at[5, j], xdn))

    @pl.loop(0, NCH)
    def _(j):
        part[j] = part[j] + mm(7, j)
        for cp in far(j):
            cp.start()

    @pl.loop(0, NCH)
    def _(j):
        for cp in near(j):
            cp.start()

    @pl.loop(0, NCH)
    def _(j):
        fa, fb = far(j)
        r_up, r_dn = relay(j)
        fa.wait_recv()
        ra1[j] = ra1[j] + part[j, tokens(1, 0), :]
        r_up.start()
        fb.wait_recv()
        rb1[j] = rb1[j] + part[j, tokens(-1, 1), :]
        r_dn.start()

    for j in range(NCH):
        nb, na = near(j)
        r_up, r_dn = relay(j)
        na.wait_recv()
        nb.wait_recv()
        r_up.wait_recv()
        r_dn.wait_recv()
        cc = pl.ds(j * CW, CW)
        logit[pl.ds(0, HALF), cc] = part[j, tokens(0, 0), :] + ra2[j] + ra3[j]
        logit[pl.ds(HALF, HALF), cc] = part[j, tokens(0, 1), :] + rb2[j] + rb3[j]

    @pl.loop(0, OWN // 32)
    def _(i):
        rows = pl.ds(pl.multiple_of(i * 32, 32), 32)
        t = logit[rows, :]
        m = jnp.max(t, axis=1, keepdims=True)
        t = t - m
        w = jnp.where(lane == 0, m, wt[rows, :])
        w = jnp.where(lane == 1, jnp.sum(jnp.exp(t), axis=1, keepdims=True), w)
        for k in range(NT):
            w = jnp.where(lane == 2 + k, jnp.sum(jnp.exp(t * inv[k]), axis=1, keepdims=True), w)
        wt[rows, :] = w

    st[0] = wt[...].T[0:16, :]

    def merge(load, n):
        sm = load(0)[0:1, :]
        tm = load(0)[8:9, :]
        for k in range(1, n):
            sm = jnp.maximum(sm, load(k)[0:1, :])
            tm = jnp.maximum(tm, load(k)[8:9, :])
        ss = [0.0] * (1 + NT)
        ts = [0.0] * NT
        for k in range(n):
            s = load(k)
            dm = s[0:1, :] - sm
            dt = s[8:9, :] - tm
            ss[0] = ss[0] + s[1:2, :] * jnp.exp(dm)
            for q in range(NT):
                ss[1 + q] = ss[1 + q] + s[2 + q:3 + q, :] * jnp.exp(dm * inv[q])
                ts[q] = ts[q] + s[9 + q:10 + q, :] * jnp.exp(dt * inv[q])
        return sm, ss, tm, ts

    def exchange(src, dst, ssem, rsem, group):
        flight = [send(src, dst.at[k], ssem.at[k], rsem.at[k], group(k)) for k in range(1, 8)]
        for f in flight:
            f.wait_recv()

    exchange(st.at[0], r1, s1_s, s1_r, group1)
    sm, ss, tm, ts = merge(lambda k: st[0] if k == 0 else r1[k], 8)
    pad = jnp.zeros((2, 256), F32)
    st[1] = jnp.concatenate([sm] + ss + [pad, tm] + ts + [jnp.zeros((3, 256), F32)], axis=0)
    exchange(st.at[1], r2, s2_s, s2_r, group2)
    sm, ss, tm, ts = merge(lambda k: st[1] if k == 0 else r2[k], 8)
    rows = [sm, mix[0] / ss[0]]
    rows += [mix[1] * temps[q] / ss[1 + q] for q in range(NT)]
    rows += [pad, tm]
    rows += [mix[1] * temps[q] / ts[q] for q in range(NT)]
    rows += [jnp.zeros((3, 256), F32)]
    ct[pl.ds(0, 16), :] = jnp.concatenate(rows, axis=0)
    ct[pl.ds(16, 112), :] = jnp.zeros((112, 256), F32)
    coef[...] = ct[...].T

    base = v * COLS
    col = lax.broadcasted_iota(jnp.int32, (32, CW), 1)

    def make_grad(j):
        @pl.loop(0, OWN // 32)
        def _(i):
            rows = pl.ds(pl.multiple_of(i * 32, 32), 32)
            cf = coef[rows, :]
            s = logit[rows, pl.ds(j * CW, CW)] - cf[:, 0:1]
            t = teach[rows, pl.ds(j * CW, CW)].astype(F32) - cf[:, 8:9]
            g = cf[:, 1:2] * jnp.exp(s)
            g = g - jnp.where(col + (base + j * CW) == labels[rows, :], mix[0], 0.0)
            for q in range(NT):
                g = g + cf[:, 2 + q:3 + q] * jnp.exp(s * inv[q])
                g = g - cf[:, 9 + q:10 + q] * jnp.exp(t * inv[q])
            out = pl.ds(pl.multiple_of(x * OWN + i * 32, 32), 32)
            grads[j, out, :] = g.astype(BF)

    def gblock(j, d):
        return grads.at[j, pl.ds(pl.multiple_of(xrel(d) * OWN, OWN), OWN)]

    def gown(j):
        b = gblock(j, 0)
        return (rcopy(b, b, gx_s.at[0, j], gx_r.at[0, j], xup),
                rcopy(b, b, gx_s.at[1, j], gx_r.at[1, j], xdn))

    def gfwd(j):
        a = grads.at[j, tokens(-1, 0)]
        b = grads.at[j, tokens(1, 1)]
        return (rcopy(a, a, gx_s.at[2, j], gx_r.at[2, j], xup),
                rcopy(b, b, gx_s.at[3, j], gx_r.at[3, j], xdn))

    def put(j):
        make_grad(j)
        for cp in gown(j):
            cp.start()

    def passon(j):
        for o, f in zip(gown(j), gfwd(j)):
            o.wait_recv()
            f.start()

    def hidden_part(j, zb):
        rows = pl.ds(pl.multiple_of(zb * 256, 256), 256)
        r = lax.dot_general(hd[j, rows, :], grads[j], (((1,), (1,)), ((), ())),
                            preferred_element_type=F32)
        return r.reshape(NY, NC, LROWS, TOK)

    def head_part(j):
        @pl.loop(0, NZ)
        def _(b):
            lhs = hb[b].reshape(256, TOK)
            r = jnp.dot(lhs, grads[j], preferred_element_type=F32)
            rows = pl.ds(pl.multiple_of(b * 256, 256), 256)
            hdgrad[rows, pl.ds(j * CW, CW)] = r.astype(BF)

    def arrive(j):
        for f in gfwd(j):
            f.wait_recv()

    put(0)
    put(1)
    passon(0)
    for j in range(NCH - 1):
        if j + 2 < NCH:
            put(j + 2)
        passon(j + 1)
        arrive(j)

        @pl.loop(0, NZ)
        def _(b):
            if j == 0:
                hg[b] = hidden_part(j, b)
            else:
                hg[b] = hg[b] + hidden_part(j, b)
        if j > 0:
            head_part(j - 1)
    last = NCH - 1
    arrive(last)

    def pair(i):
        zb = zrel(ORDER[i])
        tot = hg[zb] + hidden_part(last, zb)
        hg[zb] = tot
        ps[i] = hg[zb, :, 1 - c].astype(BF)
        return send(ps.at[i], pr.at[i], pp_s.at[i], pp_r.at[i], mate)

    pairs = {}
    for i in (7, 6, 5, 4, 3, 2, 1, 0):
        pairs[i] = pair(i)

    def total(i):
        pairs[i].wait_recv()
        return hg[zrel(ORDER[i]), :, c] + pr[i].astype(F32)

    def zhop(step, part_id, val, dev):
        zs[step, part_id] = val.astype(BF)
        return send(zs.at[step, part_id], zr.at[step, part_id],
                    zz_s.at[step, part_id], zz_r.at[step, part_id], dev)

    q4 = total(7)
    up_lo = zhop(0, 0, q4[:, :, :CH], zup)
    dn_hi = zhop(0, 3, q4[:, :, CH:], zdn)
    up_hi = dn_lo = None
    for step in range(1, 4):
        dist = 4 - step
        qu = total(2 * dist)
        qd = total(2 * dist - 1)
        nu_hi = qu[:, :, CH:]
        nd_lo = qd[:, :, :CH]
        if up_hi is not None:
            up_hi.wait_recv()
            nu_hi = nu_hi + zr[step - 1, 1].astype(F32)
            dn_lo.wait_recv()
            nd_lo = nd_lo + zr[step - 1, 2].astype(F32)
        up_hi = zhop(step, 1, nu_hi, zup)
        dn_lo = zhop(step, 2, nd_lo, zdn)
        up_lo.wait_recv()
        nu_lo = qu[:, :, :CH] + zr[step - 1, 0].astype(F32)
        up_lo = zhop(step, 0, nu_lo, zup)
        dn_hi.wait_recv()
        nd_hi = qd[:, :, CH:] + zr[step - 1, 3].astype(F32)
        dn_hi = zhop(step, 3, nd_hi, zdn)
        if step < 3:
            head_part(last - 2 + step)

    q0 = total(0)
    up_hi.wait_recv()
    dn_lo.wait_recv()
    up_lo.wait_recv()
    dn_hi.wait_recv()
    own_lo = q0[:, :, :CH] + zr[3, 0].astype(F32) + zr[3, 2].astype(F32)
    own_hi = q0[:, :, CH:] + zr[3, 1].astype(F32) + zr[3, 3].astype(F32)
    ysb[0] = own_lo
    ysb[1] = own_hi

    fa = send(ysb.at[0, yrel(2)], yrb.at[0], yy_s.at[0], yy_r.at[0], yup)
    fb = send(ysb.at[1, yrel(2)], yrb.at[1], yy_s.at[1], yy_r.at[1], ydn)
    nb = send(ysb.at[1, yrel(1)], yrb.at[2], yy_s.at[2], yy_r.at[2], yup)
    na = send(ysb.at[0, yrel(-1)], yrb.at[3], yy_s.at[3], yy_r.at[3], ydn)
    fa.wait_recv()
    yrb[0] = yrb[0] + ysb[0, yrel(1)]
    ga = send(yrb.at[0], yrb.at[4], yy_s.at[4], yy_r.at[4], yup)
    fb.wait_recv()
    yrb[1] = yrb[1] + ysb[1, yrel(-1)]
    gb = send(yrb.at[1], yrb.at[5], yy_s.at[5], yy_r.at[5], ydn)
    na.wait_recv()
    nb.wait_recv()
    ga.wait_recv()
    gb.wait_recv()
    hgrad[:, pl.ds(0, CH)] = ysb[0, y] + yrb[3] + yrb[4]
    hgrad[:, pl.ds(CH, CH)] = ysb[1, y] + yrb[2] + yrb[5]

    for cp in sent:
        cp.wait_send()

    @pl.loop(0, NCH)
    def _(j):
        for cp in far(j) + near(j) + relay(j) + gown(j) + gfwd(j):
            cp.wait_send()


def shards(hidden_t, head, teacher, labels, temps, mix):
    vmem = pl.BlockSpec(memory_space=pltpu.VMEM)
    smem = pl.BlockSpec(memory_space=pltpu.SMEM)
    hbm = pl.BlockSpec(memory_space=pl.ANY)
    dma = pltpu.SemaphoreType.DMA
    half = (NCH, HALF, CW)
    return pl.pallas_call(
        body,
        out_shape=(
            jax.ShapeDtypeStruct((LROWS, TOK), F32),
            jax.ShapeDtypeStruct((FEAT, COLS), BF),
        ),
        in_specs=[vmem, hbm, hbm, vmem, smem, smem],
        out_specs=(vmem, vmem),
        scratch_shapes=[
            pltpu.VMEM((NZ, NY, NC, LROWS, TOK), BF),
            pltpu.VMEM((NCH, FEAT, CW), BF),
            pltpu.VMEM((8, TOK, 256), BF),
            pltpu.VMEM((NCH, TOK, CW), F32),
            pltpu.VMEM(half, F32), pltpu.VMEM(half, F32),
            pltpu.VMEM(half, F32), pltpu.VMEM(half, F32),
            pltpu.VMEM(half, F32), pltpu.VMEM(half, F32),
            pltpu.VMEM((OWN, COLS), F32),
            pltpu.VMEM((OWN, COLS), BF),
            pltpu.VMEM((256, 128), F32),
            pltpu.VMEM((2, 16, 256), F32),
            pltpu.VMEM((8, 16, 256), F32),
            pltpu.VMEM((8, 16, 256), F32),
            pltpu.VMEM((128, 256), F32),
            pltpu.VMEM((256, 128), F32),
            pltpu.VMEM((NCH, TOK, CW), BF),
            pltpu.VMEM((NZ, NY, NC, LROWS, TOK), F32),
            pltpu.VMEM((8, NY, LROWS, TOK), BF),
            pltpu.VMEM((8, NY, LROWS, TOK), BF),
            pltpu.VMEM((4, 4, NY, LROWS, CH), BF),
            pltpu.VMEM((4, 4, NY, LROWS, CH), BF),
            pltpu.VMEM((2, NY, LROWS, CH), F32),
            pltpu.VMEM((6, LROWS, CH), F32),
            dma((NCH + 1,)), dma,
            dma((4,)), dma((4,)),
            dma((8,)), dma((8,)),
            dma((8,)), dma((8,)),
            dma((6, NCH)), dma((6, NCH)),
            dma((8,)), dma((8,)),
            dma((8,)), dma((8,)),
            dma((4, NCH)), dma((4, NCH)),
            dma((8,)), dma((8,)),
            dma((4, 4)), dma((4, 4)),
            dma((6,)), dma((6,)),
        ],
        compiler_params=pltpu.CompilerParams(
            collective_id=0, has_side_effects=True, vmem_limit_bytes=60 * 1024 * 1024
        ),
    )(hidden_t, head, teacher, labels.reshape(OWN, 1), temps, mix)


def solution(mesh):
    placed = (P(("dp", "vocab"), None), P("dp", "vocab"), P("dp", "vocab"), P("dp"), P(), P())
    return jax.shard_map(
        shards,
        mesh=mesh,
        in_specs=placed,
        out_specs=(P(("dp", "vocab"), None), P("dp", "vocab")),
        check_vma=False,
    )
```

```python
import jax
import jax.numpy as jnp
from jax import lax
from jax.experimental import pallas as pl
from jax.experimental.pallas import tpu as pltpu
from jax.sharding import PartitionSpec as P

BF = jnp.bfloat16
F32 = jnp.float32
MESH = pl.DeviceIdType.MESH
NX, NZ, NY, NC = 4, 8, 4, 2
TOK, OWN = 768, 192
K = 3
CT = TOK // K
GT = CT // NX
GH = GT // 2
LH = CT // 2
COLS, CW, NCH = 1280, 256, 5
FEAT, LROWS = 2048, 32
NT = 4
ORDER = (0, -1, 1, -2, 2, -3, 3, 4)


def body(hid, head_hbm, teach_hbm, labels, temps, mix,
         hgrad, hdgrad,
         hb, hd, ht, part, ra1, rb1, ra2, rb2, ra3, rb3, logit, teach,
         wt, st, r1, r2, ct, coef, lab, grads, tmp, hgo, ps, pr, zs, zr, ysb, yrb, res,
         loc_sem, ay_s, ay_r, az_s, az_r, ap_s, ap_r,
         rx_s, rx_r, s1_s, s1_r, s2_s, s2_r, gx_s, gx_r,
         pp_s, pp_r, zz_s, zz_r, yy_s, yy_r):
    x = lax.axis_index("dp")
    v = lax.axis_index("vocab")
    c = lax.rem(v, 2)
    y = lax.rem(v // 2, NY)
    z = v // (NY * NC)

    def vid(zz, yy, cc):
        return {"vocab": (zz * NY + yy) * NC + cc}

    def zrel(d):
        return lax.rem(z + (d + NZ), NZ)

    def yrel(d):
        return lax.rem(y + (d + NY), NY)

    def xrel(d):
        return lax.rem(x + (d + NX), NX)

    zup, zdn = vid(zrel(1), y, c), vid(zrel(-1), y, c)
    yup, ydn = vid(z, yrel(1), c), vid(z, yrel(-1), c)
    mate = vid(z, y, 1 - c)
    xup, xdn = {"dp": xrel(1)}, {"dp": xrel(-1)}
    slot = y * NC + c

    def group1(k):
        other = lax.rem(slot + k, 8)
        return vid(z, other // NC, lax.rem(other, NC))

    def group2(k):
        return vid(zrel(k), y, c)

    sent = []

    def send(src, dst, ssem, rsem, dev):
        cp = pltpu.make_async_remote_copy(
            src_ref=src, dst_ref=dst, send_sem=ssem, recv_sem=rsem,
            device_id=dev, device_id_type=MESH)
        cp.start()
        sent.append(cp)
        return cp

    bar = pltpu.get_barrier_semaphore()
    for k in range(1, 8):
        pl.semaphore_signal(bar, inc=1, device_id=group1(k), device_id_type=MESH)
        pl.semaphore_signal(bar, inc=1, device_id=group2(k), device_id_type=MESH)
    pl.semaphore_signal(bar, inc=1, device_id=xup, device_id_type=MESH)
    pl.semaphore_signal(bar, inc=1, device_id=xdn, device_id_type=MESH)

    head_copy = pltpu.make_async_copy(head_hbm, hd, loc_sem.at[0])
    head_copy.start()
    teach_copy = pltpu.make_async_copy(teach_hbm, teach, loc_sem.at[1])
    teach_copy.start()

    h32 = hid[...].astype(F32)
    for k in range(K):
        piece = jnp.concatenate(
            [h32[:, d * OWN + k * GT:d * OWN + (k + 1) * GT] for d in range(NX)], axis=1)
        hb[z, y, c, :, pl.ds(k * CT, CT)] = piece.astype(BF)

    pl.semaphore_wait(bar, 16)

    lo, hi = pl.ds(0, TOK // 2), pl.ds(TOK // 2, TOK // 2)
    own = hb.at[z, y, c]
    y0 = send(own, own, ay_s.at[0], ay_r.at[0], yup)
    y1 = send(own, own, ay_s.at[1], ay_r.at[1], ydn)

    inv = [1.0 / temps[q] for q in range(NT)]
    lane = lax.broadcasted_iota(jnp.int32, (32, 128), 1)
    row3 = lax.broadcasted_iota(jnp.int32, (2, 8, 1), 1)
    blk3 = lax.broadcasted_iota(jnp.int32, (2, 8, 1), 0)
    invc = jnp.zeros((2, 8, 1), F32)
    wcol = jnp.zeros((2, 8, 1), F32)
    invc = jnp.where((blk3 == 0) & (row3 == 1), 1.0, invc)
    wcol = jnp.where((blk3 == 0) & (row3 == 1), mix[0], wcol)
    for q in range(NT):
        hit = ((blk3 == 0) & (row3 == 2 + q)) | ((blk3 == 1) & (row3 == 1 + q))
        invc = jnp.where(hit, inv[q], invc)
        wcol = jnp.where(hit, mix[1] * temps[q], wcol)

    lab[...] = jnp.zeros((256, 128), F32)
    labrow = jnp.concatenate(
        [labels[...].astype(F32), jnp.zeros((1, 256 - OWN), F32)], axis=1)
    lab[...] = jnp.broadcast_to(labrow, (128, 256)).T

    y0.wait_recv()
    fw = hb.at[z, yrel(-1), c, :, lo]
    y2 = send(fw, fw, ay_s.at[2], ay_r.at[2], yup)
    y1.wait_recv()
    fw = hb.at[z, yrel(1), c, :, hi]
    y3 = send(fw, fw, ay_s.at[3], ay_r.at[3], ydn)

    teach_copy.wait()

    def teacher_stats(k):
        @pl.loop(0, GT // 32)
        def _(i):
            r = pl.ds(pl.multiple_of(i * 32, 32), 32)
            t = teach[pl.ds(pl.multiple_of(k * GT + i * 32, 32), 32), :].astype(F32)
            m = jnp.max(t, axis=1, keepdims=True)
            t = t - m
            w = jnp.where(lane == 8, m, 0.0)
            for q in range(NT):
                w = jnp.where(lane == 9 + q, jnp.sum(jnp.exp(t * inv[q]), axis=1, keepdims=True), w)
            wt[k, r, :] = w

        wt[k, pl.ds(GT, 128 - GT), :] = jnp.zeros((128 - GT, 128), F32)

    teacher_stats(0)
    y2.wait_recv()
    y3.wait_recv()

    def zsend(k, d, step):
        ck = pl.ds(k * CT, CT)
        if step < 4:
            up = hb.at[zrel(-d), :, c, :, ck]
            dn = hb.at[zrel(d), :, c, :, ck]
        else:
            up = hb.at[zrel(-d), :, c, :, pl.ds(k * CT, LH)]
            dn = hb.at[zrel(d), :, c, :, pl.ds(k * CT + LH, LH)]
        a, b = 2 * step - 2, 2 * step - 1
        return (send(up, up, az_s.at[k, a], az_r.at[k, a], zup),
                send(dn, dn, az_s.at[k, b], az_r.at[k, b], zdn))

    gives = {}

    def give(k, i):
        b = hb.at[zrel(ORDER[i]), :, c, :, pl.ds(k * CT, CT)]
        gives[k, i] = send(b, b, ap_s.at[k, i], ap_r.at[k, i], mate)

    def stage(k, ids):
        for i in ids:
            gives[k, i].wait_recv()
            blk = hb[zrel(ORDER[i]), :, :, :, pl.ds(k * CT, CT)].reshape(256, CT)
            ht[i] = blk.T

        @pl.loop(0, NCH)
        def _(j):
            cc = pl.ds(pl.multiple_of(j * CW, CW), CW)
            acc = None
            for i in ids:
                rows = pl.ds(pl.multiple_of(zrel(ORDER[i]) * 256, 256), 256)
                t = jnp.dot(ht[i], hd[rows, cc], preferred_element_type=F32)
                acc = t if acc is None else acc + t
            if ids[0] != 0:
                acc = acc + part[k, :, cc]
            part[k, :, cc] = acc

    flights = {}

    def zstart(k):
        flights[k] = zsend(k, 0, 1)
        give(k, 0)

    def advance(k, s):
        for f in flights[k]:
            f.wait_recv()
        if s < 4:
            flights[k] = zsend(k, s, s + 1)
            give(k, 2 * s - 1)
            give(k, 2 * s)
        else:
            give(k, 7)

    STAGES = {1: [0, 1, 2], 2: [3, 4], 3: [5, 6], 4: [7]}

    def tokens(d, half):
        return pl.ds(pl.multiple_of(xrel(d) * GT + half * GH, GH), GH)

    flying = {}

    def far(k):
        flying[k, 0] = send(part.at[k, tokens(2, 0)], ra1.at[k], rx_s.at[k, 0], rx_r.at[k, 0], xup)
        flying[k, 1] = send(part.at[k, tokens(2, 1)], rb1.at[k], rx_s.at[k, 1], rx_r.at[k, 1], xdn)

    def near(k):
        flying[k, 2] = send(part.at[k, tokens(1, 1)], rb2.at[k], rx_s.at[k, 2], rx_r.at[k, 2], xup)
        flying[k, 3] = send(part.at[k, tokens(-1, 0)], ra2.at[k], rx_s.at[k, 3], rx_r.at[k, 3], xdn)

    def relay(k):
        flying[k, 0].wait_recv()
        ra1[k] = ra1[k] + part[k, tokens(1, 0), :]
        flying[k, 4] = send(ra1.at[k], ra3.at[k], rx_s.at[k, 4], rx_r.at[k, 4], xup)
        flying[k, 1].wait_recv()
        rb1[k] = rb1[k] + part[k, tokens(-1, 1), :]
        flying[k, 5] = send(rb1.at[k], rb3.at[k], rx_s.at[k, 5], rx_r.at[k, 5], xdn)

    def final(k):
        for i in (2, 3, 4, 5):
            flying[k, i].wait_recv()
        logit[pl.ds(k * GT, GH), :] = part[k, tokens(0, 0), :] + ra2[k] + ra3[k]
        logit[pl.ds(k * GT + GH, GH), :] = part[k, tokens(0, 1), :] + rb2[k] + rb3[k]

    swaps = {}

    def exchange(k, src, dst, ssem, rsem, group):
        swaps[k] = [send(src, dst.at[k, i], ssem.at[k, i], rsem.at[k, i], group(i))
                    for i in range(1, 8)]

    def local_stats(k):
        @pl.loop(0, GT // 32)
        def _(i):
            r = pl.ds(pl.multiple_of(i * 32, 32), 32)
            t = logit[pl.ds(pl.multiple_of(k * GT + i * 32, 32), 32), :]
            m = jnp.max(t, axis=1, keepdims=True)
            t = t - m
            w = jnp.where(lane == 0, m, wt[k, r, :])
            w = jnp.where(lane == 1, jnp.sum(jnp.exp(t), axis=1, keepdims=True), w)
            for q in range(NT):
                w = jnp.where(lane == 2 + q, jnp.sum(jnp.exp(t * inv[q]), axis=1, keepdims=True), w)
            wt[k, r, :] = w

        st[k, 0] = wt[k].T[0:16, :]
        exchange(k, st.at[k, 0], r1, s1_s, s1_r, group1)

    def merge(k, mine, got):
        for f in swaps[k]:
            f.wait_recv()
        all_s = [st[k, mine].reshape(2, 8, 128)]
        all_s += [got[k, i].reshape(2, 8, 128) for i in range(1, 8)]
        top = all_s[0][:, 0:1, :]
        for s in all_s[1:]:
            top = jnp.maximum(top, s[:, 0:1, :])
        acc = None
        for s in all_s:
            t = s * jnp.exp((s[:, 0:1, :] - top) * invc)
            acc = t if acc is None else acc + t
        return top, acc

    def merge1(k):
        top, acc = merge(k, 0, r1)
        st[k, 1] = jnp.where(row3 == 0, top, acc).reshape(16, 128)
        exchange(k, st.at[k, 1], r2, s2_s, s2_r, group2)

    base = v * COLS
    col = lax.broadcasted_iota(jnp.int32, (32, CW), 1).astype(F32)

    def grad(k):
        top, acc = merge(k, 1, r2)
        acc = jnp.where(wcol > 0.0, acc, 1.0)
        ct[pl.ds(0, 16), :] = jnp.where(row3 == 0, top, wcol / acc).reshape(16, 128)
        ct[pl.ds(16, 112), :] = jnp.zeros((112, 128), F32)
        coef[...] = ct[...].T

        for i in range(GT // 32):
            cf = coef[pl.ds(i * 32, 32), :]
            r = pl.ds(k * GT + i * 32, 32)
            lb = lab[r, 0:1]

            @pl.loop(0, NCH)
            def _(j):
                cc = pl.ds(pl.multiple_of(j * CW, CW), CW)
                s = logit[r, cc] - cf[:, 0:1]
                t = teach[r, cc].astype(F32) - cf[:, 8:9]
                g = cf[:, 1:2] * jnp.exp(s)
                g = g - jnp.where(col + (base + j * CW).astype(F32) == lb, mix[0], 0.0)
                for q in range(NT):
                    g = g + cf[:, 2 + q:3 + q] * jnp.exp(s * inv[q])
                    g = g - cf[:, 9 + q:10 + q] * jnp.exp(t * inv[q])
                out = pl.ds(pl.multiple_of(k * CT + x * GT + i * 32, 32), 32)
                grads[out, cc] = g.astype(BF)

        b = grads.at[pl.ds(pl.multiple_of(k * CT + x * GT, GT), GT)]
        flying[k, 6] = send(b, b, gx_s.at[k, 0], gx_r.at[k, 0], xup)
        flying[k, 7] = send(b, b, gx_s.at[k, 1], gx_r.at[k, 1], xdn)

    def passon(k):
        a = grads.at[pl.ds(pl.multiple_of(k * CT + xrel(-1) * GT, GH), GH)]
        b = grads.at[pl.ds(pl.multiple_of(k * CT + xrel(1) * GT + GH, GH), GH)]
        flying[k, 6].wait_recv()
        flying[k, 8] = send(a, a, gx_s.at[k, 2], gx_r.at[k, 2], xup)
        flying[k, 7].wait_recv()
        flying[k, 9] = send(b, b, gx_s.at[k, 3], gx_r.at[k, 3], xdn)

    pairs = {}

    def pair(k, i):
        zb = zrel(ORDER[i])
        rows = pl.ds(pl.multiple_of(zb * 256, 256), 256)
        r = lax.dot_general(hd[rows, :], grads[pl.ds(k * CT, CT), :], (((1,), (1,)), ((), ())),
                            preferred_element_type=F32)
        tmp[...] = r.reshape(NY, NC, LROWS, CT)
        hgo[k, i] = tmp[:, c]
        ps[k, i] = tmp[:, 1 - c].astype(BF)
        pairs[k, i] = send(ps.at[k, i], pr.at[k, i], pp_s.at[k, i], pp_r.at[k, i], mate)

    def total(k, i):
        pairs[k, i].wait_recv()
        return hgo[k, i] + pr[k, i].astype(F32)

    hops = {}

    def zhop(k, step, lane_id, val, dev):
        zs[k, step, lane_id] = val.astype(BF)
        hops[k, lane_id] = send(zs.at[k, step, lane_id], zr.at[k, step, lane_id],
                                zz_s.at[k, step, lane_id], zz_r.at[k, step, lane_id], dev)

    def got(k, step, lane_id):
        hops[k, lane_id].wait_recv()
        return zr[k, step, lane_id].astype(F32)

    def yhop(k, i, src, dev):
        hops[k, "y", i] = send(src, yrb.at[k, i], yy_s.at[k, i], yy_r.at[k, i], dev)

    def scatter(k, step):
        if step == 0:
            q4 = total(k, 7)
            zhop(k, 0, 0, q4[:, :, :LH], zup)
            zhop(k, 0, 3, q4[:, :, LH:], zdn)
        elif step < 4:
            dist = 4 - step
            qu = total(k, 2 * dist)
            qd = total(k, 2 * dist - 1)
            nu_hi, nd_lo = qu[:, :, LH:], qd[:, :, :LH]
            if step > 1:
                nu_hi = nu_hi + got(k, step - 1, 1)
                nd_lo = nd_lo + got(k, step - 1, 2)
            zhop(k, step, 1, nu_hi, zup)
            zhop(k, step, 2, nd_lo, zdn)
            zhop(k, step, 0, qu[:, :, :LH] + got(k, step - 1, 0), zup)
            zhop(k, step, 3, qd[:, :, LH:] + got(k, step - 1, 3), zdn)
        elif step == 4:
            q0 = total(k, 0)
            ysb[k, 0] = q0[:, :, :LH] + got(k, 3, 0) + got(k, 3, 2)
            ysb[k, 1] = q0[:, :, LH:] + got(k, 3, 1) + got(k, 3, 3)
            yhop(k, 0, ysb.at[k, 0, yrel(2)], yup)
            yhop(k, 1, ysb.at[k, 1, yrel(2)], ydn)
            yhop(k, 2, ysb.at[k, 1, yrel(1)], yup)
            yhop(k, 3, ysb.at[k, 0, yrel(-1)], ydn)
        elif step == 5:
            hops[k, "y", 0].wait_recv()
            yrb[k, 0] = yrb[k, 0] + ysb[k, 0, yrel(1)]
            yhop(k, 4, yrb.at[k, 0], yup)
            hops[k, "y", 1].wait_recv()
            yrb[k, 1] = yrb[k, 1] + ysb[k, 1, yrel(-1)]
            yhop(k, 5, yrb.at[k, 1], ydn)
        else:
            for i in (2, 3, 4, 5):
                hops[k, "y", i].wait_recv()
            res[k, :, pl.ds(0, LH)] = ysb[k, 0, y] + yrb[k, 3] + yrb[k, 4]
            res[k, :, pl.ds(LH, LH)] = ysb[k, 1, y] + yrb[k, 2] + yrb[k, 5]

    def head_part(b):
        lhs = hb[b].reshape(256, TOK)

        @pl.loop(0, NCH)
        def _(j):
            cc = pl.ds(pl.multiple_of(j * CW, CW), CW)
            r = jnp.dot(lhs, grads[:, cc], preferred_element_type=F32)
            hdgrad[pl.ds(b * 256, 256), cc] = r.astype(BF)

    zstart(0)
    teacher_stats(1)
    head_copy.wait()
    for t in range(8):
        for k in range(K):
            s = t - 2 * k + 1
            if 1 <= s <= 4:
                advance(k, s)
        if t in (1, 3):
            zstart((t + 1) // 2)
        for k in range(K):
            s = t - 2 * k + 1
            if 1 <= s <= 4:
                stage(k, STAGES[s])
                if s == 4:
                    far(k)
                    if k > 0:
                        relay(k - 1)
                    near(k)
        if t == 2:
            teacher_stats(2)

    final(0)
    local_stats(0)
    merge1(0)
    relay(2)
    final(1)
    local_stats(1)
    grad(0)
    merge1(1)
    final(2)
    local_stats(2)
    grad(1)
    passon(0)
    merge1(2)
    passon(1)
    for i in (8, 9):
        flying[0, i].wait_recv()
    for i in (7, 6, 5, 4):
        pair(0, i)
    grad(2)
    for i in (3, 2, 1, 0):
        pair(0, i)
    scatter(0, 0)
    for i in (8, 9):
        flying[1, i].wait_recv()
    passon(2)
    for i in (7, 6, 5, 4):
        pair(1, i)
    scatter(0, 1)
    for i in (3, 2, 1, 0):
        pair(1, i)
    scatter(1, 0)
    for i in (8, 9):
        flying[2, i].wait_recv()
    pair(2, 7)
    pair(2, 6)
    pair(2, 5)
    scatter(2, 0)
    for i in (4, 3, 2, 1, 0):
        pair(2, i)
    scatter(1, 1)
    scatter(0, 2)
    for t in range(1, 7):
        scatter(2, t)
        if t + 1 < 7:
            scatter(1, t + 1)
        if t + 2 < 7:
            scatter(0, t + 2)
        for b in {1: (0, 1), 2: (2, 3), 3: (4, 5), 4: (6,), 5: (7,)}.get(t, ()):
            head_part(b)

    full = [res[k] for k in range(K)]
    hgrad[...] = jnp.concatenate(
        [full[k][:, d * GT:(d + 1) * GT] for d in range(NX) for k in range(K)], axis=1)

    for cp in sent:
        cp.wait_send()


def shards(hidden_t, head, teacher, labels, temps, mix):
    vmem = pl.BlockSpec(memory_space=pltpu.VMEM)
    smem = pl.BlockSpec(memory_space=pltpu.SMEM)
    hbm = pl.BlockSpec(memory_space=pl.ANY)
    dma = pltpu.SemaphoreType.DMA
    half = (K, GH, COLS)
    return pl.pallas_call(
        body,
        out_shape=(
            jax.ShapeDtypeStruct((LROWS, TOK), F32),
            jax.ShapeDtypeStruct((FEAT, COLS), BF),
        ),
        in_specs=[vmem, hbm, hbm, vmem, smem, smem],
        out_specs=(vmem, vmem),
        scratch_shapes=[
            pltpu.VMEM((NZ, NY, NC, LROWS, TOK), BF),
            pltpu.VMEM((FEAT, COLS), BF),
            pltpu.VMEM((8, CT, 256), BF),
            pltpu.VMEM((K, CT, COLS), F32),
            pltpu.VMEM(half, F32), pltpu.VMEM(half, F32),
            pltpu.VMEM(half, F32), pltpu.VMEM(half, F32),
            pltpu.VMEM(half, F32), pltpu.VMEM(half, F32),
            pltpu.VMEM((OWN, COLS), F32),
            pltpu.VMEM((OWN, COLS), BF),
            pltpu.VMEM((K, 128, 128), F32),
            pltpu.VMEM((K, 2, 16, 128), F32),
            pltpu.VMEM((K, 8, 16, 128), F32),
            pltpu.VMEM((K, 8, 16, 128), F32),
            pltpu.VMEM((128, 128), F32),
            pltpu.VMEM((128, 128), F32),
            pltpu.VMEM((256, 128), F32),
            pltpu.VMEM((TOK, COLS), BF),
            pltpu.VMEM((NY, NC, LROWS, CT), F32),
            pltpu.VMEM((K, 8, NY, LROWS, CT), F32),
            pltpu.VMEM((K, 8, NY, LROWS, CT), BF),
            pltpu.VMEM((K, 8, NY, LROWS, CT), BF),
            pltpu.VMEM((K, 4, 4, NY, LROWS, LH), BF),
            pltpu.VMEM((K, 4, 4, NY, LROWS, LH), BF),
            pltpu.VMEM((K, 2, NY, LROWS, LH), F32),
            pltpu.VMEM((K, 6, LROWS, LH), F32),
            pltpu.VMEM((K, LROWS, CT), F32),
            dma((2,)),
            dma((4,)), dma((4,)),
            dma((K, 8)), dma((K, 8)),
            dma((K, 8)), dma((K, 8)),
            dma((K, 6)), dma((K, 6)),
            dma((K, 8)), dma((K, 8)),
            dma((K, 8)), dma((K, 8)),
            dma((K, 4)), dma((K, 4)),
            dma((K, 8)), dma((K, 8)),
            dma((K, 4, 4)), dma((K, 4, 4)),
            dma((K, 6)), dma((K, 6)),
        ],
        compiler_params=pltpu.CompilerParams(
            collective_id=0, has_side_effects=True, vmem_limit_bytes=56 * 1024 * 1024
        ),
    )(hidden_t, head, teacher, labels.reshape(1, OWN), temps, mix)


def solution(mesh):
    placed = (P(("dp", "vocab"), None), P("dp", "vocab"), P("dp", "vocab"), P("dp"), P(), P())
    return jax.shard_map(
        shards,
        mesh=mesh,
        in_specs=placed,
        out_specs=(P(("dp", "vocab"), None), P("dp", "vocab")),
        check_vma=False,
    )
```

```python
import jax
import jax.numpy as jnp
from jax import lax
from jax.experimental import pallas as pl
from jax.experimental.pallas import tpu as pltpu
from jax.sharding import PartitionSpec as P

BF = jnp.bfloat16
F32 = jnp.float32
MESH = pl.DeviceIdType.MESH
NX, NZ, NY, NC = 4, 8, 4, 2
TOK, OWN = 768, 192
K = 3
CT = TOK // K
GT = CT // NX
GH = GT // 2
LH = CT // 2
COLS, CW, NCH = 1280, 256, 5
FEAT, LROWS = 2048, 32
NT = 4
GATHER = (0, -1, 1, 2)
SPREAD = (2, 1, -1, 0)


def body(hid_hbm, head_hbm, teach_hbm, labels_hbm, temps_hbm, mix_hbm,
         hgrad, hdgrad,
         hid, labels, temps, mix, hdo,
         hb, hd, ht, part, ra1, rb1, ra2, rb2, ra3, rb3, logit, teach,
         wt, st, r1, r2, ct, coef, lab, grads, tmp, hgo, ps, pr, ysb, yrb, ysum, zsb, zrb, res,
         loc_sem, out_sem, fy_s, fy_r, ay_s, ay_r, az_s, az_r, ap_s, ap_r,
         rx_s, rx_r, s1_s, s1_r, s2_s, s2_r, gx_s, gx_r,
         pp_s, pp_r, zz_s, zz_r, yy_s, yy_r):
    x = lax.axis_index("dp")
    v = lax.axis_index("vocab")
    c = lax.rem(v, 2)
    y = lax.rem(v // 2, NY)
    z = v // (NY * NC)

    def vid(zz, yy, cc):
        return {"vocab": (zz * NY + yy) * NC + cc}

    def zrel(d):
        return lax.rem(z + (d + NZ), NZ)

    def yrel(d):
        return lax.rem(y + (d + NY), NY)

    def xrel(d):
        return lax.rem(x + (d + NX), NX)

    yup, ydn = vid(z, yrel(1), c), vid(z, yrel(-1), c)
    mate = vid(z, y, 1 - c)
    xup, xdn = {"dp": xrel(1)}, {"dp": xrel(-1)}
    slot = y * NC + c

    def group1(k):
        other = lax.rem(slot + k, 8)
        return vid(z, other // NC, lax.rem(other, NC))

    def group2(k):
        return vid(zrel(k), y, c)

    sent = []

    def send(src, dst, ssem, rsem, dev):
        cp = pltpu.make_async_remote_copy(
            src_ref=src, dst_ref=dst, send_sem=ssem, recv_sem=rsem,
            device_id=dev, device_id_type=MESH)
        cp.start()
        sent.append(cp)
        return cp

    small = []
    for n, (a, b) in enumerate(((hid_hbm, hid), (labels_hbm, labels), (temps_hbm, temps), (mix_hbm, mix))):
        cp = pltpu.make_async_copy(a, b, loc_sem.at[2 + n])
        cp.start()
        small.append(cp)

    bar = pltpu.get_barrier_semaphore()
    for k in range(4, 0, -1):
        for i in {4: (4,)}.get(k, (k, NZ - k)):
            pl.semaphore_signal(bar, inc=1, device_id=group2(i), device_id_type=MESH)
    for k in range(1, 8):
        pl.semaphore_signal(bar, inc=1, device_id=group1(k), device_id_type=MESH)
    pl.semaphore_signal(bar, inc=1, device_id=xup, device_id_type=MESH)
    pl.semaphore_signal(bar, inc=1, device_id=xdn, device_id_type=MESH)

    head_copy = pltpu.make_async_copy(head_hbm, hd, loc_sem.at[0])
    head_copy.start()
    teach_copy = pltpu.make_async_copy(teach_hbm, teach, loc_sem.at[1])
    teach_copy.start()

    for cp in small:
        cp.wait()

    h32 = hid[...].astype(F32)
    for k in range(K):
        piece = jnp.concatenate(
            [h32[:, d * OWN + k * GT:d * OWN + (k + 1) * GT] for d in range(NX)], axis=1)
        hb[k, z, y, c] = piece.astype(BF)

    pl.semaphore_wait(bar, 16)

    zin = {}
    fin = {}

    def zsend(k):
        own = hb.at[k, z, y, c]
        for i in range(1, NZ):
            zin[k, i] = send(own, own, az_s.at[k, i], az_r.at[k, i], group2(i))

    def piece_out(i):
        b = hb.at[0, zrel(-i), y, c]
        fin[i, 0] = send(b, b, fy_s.at[i, 0], fy_r.at[i, 0], yup)
        fin[i, 1] = send(b, b, fy_s.at[i, 1], fy_r.at[i, 1], ydn)

    def piece_on(i):
        fin[i, 0].wait_recv()
        b = hb.at[0, zrel(-i), yrel(-1), c, :, pl.ds(0, LH)]
        fin[i, 2] = send(b, b, fy_s.at[i, 2], fy_r.at[i, 2], yup)
        fin[i, 1].wait_recv()
        b = hb.at[0, zrel(-i), yrel(1), c, :, pl.ds(LH, LH)]
        fin[i, 3] = send(b, b, fy_s.at[i, 3], fy_r.at[i, 3], ydn)

    zsend(0)
    piece_out(0)

    inv = [1.0 / temps[q] for q in range(NT)]
    lane = lax.broadcasted_iota(jnp.int32, (32, 128), 1)
    row2 = lax.broadcasted_iota(jnp.int32, (8, 128), 0)
    left = lax.broadcasted_iota(jnp.int32, (8, 128), 1) < 64
    invc = jnp.where(left & (row2 == 1), 1.0, 0.0)
    wcol = jnp.where(left & (row2 == 1), mix[0], 0.0)
    for q in range(NT):
        hit = (left & (row2 == 2 + q)) | (jnp.logical_not(left) & (row2 == 1 + q))
        invc = jnp.where(hit, inv[q], invc)
        wcol = jnp.where(hit, mix[1] * temps[q], wcol)

    lab[...] = jnp.zeros((256, 128), F32)
    labrow = jnp.concatenate(
        [labels[...].astype(F32), jnp.zeros((1, 256 - OWN), F32)], axis=1)
    lab[...] = jnp.broadcast_to(labrow, (128, 256)).T

    teach_copy.wait()

    def teacher_stats(k):
        @pl.loop(0, GT // 32)
        def _(i):
            r = pl.ds(pl.multiple_of(i * 32, 32), 32)
            t = teach[pl.ds(pl.multiple_of(k * GT + i * 32, 32), 32), :].astype(F32)
            m = jnp.max(t, axis=1, keepdims=True)
            t = t - m
            w = jnp.where(lane == 8, m, 0.0)
            for q in range(NT):
                w = jnp.where(lane == 9 + q, jnp.sum(jnp.exp(t * inv[q]), axis=1, keepdims=True), w)
            wt[k, r, :] = w

        wt[k, pl.ds(GT, 128 - GT), :] = jnp.zeros((128 - GT, 128), F32)

    teacher_stats(0)

    yin = {}
    gives = {}

    def bundle(k, d):
        return hb.at[k, :, yrel(d), c]

    def give(k, i):
        b = bundle(k, GATHER[i])
        gives[k, i] = send(b, b, ap_s.at[k, i], ap_r.at[k, i], mate)

    def yfirst(k):
        for i in range(1, NZ):
            zin[k, i].wait_recv()
        b = bundle(k, 0)
        yin[k, 0] = send(b, b, ay_s.at[k, 0], ay_r.at[k, 0], yup)
        yin[k, 1] = send(b, b, ay_s.at[k, 1], ay_r.at[k, 1], ydn)
        give(k, 0)

    def ysecond(k):
        yin[k, 0].wait_recv()
        b = hb.at[k, :, yrel(-1), c, :, pl.ds(0, LH)]
        yin[k, 2] = send(b, b, ay_s.at[k, 2], ay_r.at[k, 2], yup)
        yin[k, 1].wait_recv()
        b = hb.at[k, :, yrel(1), c, :, pl.ds(LH, LH)]
        yin[k, 3] = send(b, b, ay_s.at[k, 3], ay_r.at[k, 3], ydn)
        give(k, 1)
        give(k, 2)

    def ythird(k):
        yin[k, 2].wait_recv()
        yin[k, 3].wait_recv()
        give(k, 3)

    def stage(k, i):
        gives[k, i].wait_recv()
        yb = yrel(GATHER[i])
        ht[...] = hb[k, :, yb].reshape(512, CT).T

        for j in range(NCH):
            cc = pl.ds(j * CW, CW)
            acc = jnp.dot(ht[...], hd[:, yb, :, cc].reshape(512, CW), preferred_element_type=F32)
            if i != 0:
                acc = acc + part[k, :, cc]
            part[k, :, cc] = acc

    def tokens(d, half):
        return pl.ds(pl.multiple_of(xrel(d) * GT + half * GH, GH), GH)

    flying = {}

    def far(k):
        flying[k, 0] = send(part.at[k, tokens(2, 0)], ra1.at[k], rx_s.at[k, 0], rx_r.at[k, 0], xup)
        flying[k, 1] = send(part.at[k, tokens(2, 1)], rb1.at[k], rx_s.at[k, 1], rx_r.at[k, 1], xdn)

    def near(k):
        flying[k, 2] = send(part.at[k, tokens(1, 1)], rb2.at[k], rx_s.at[k, 2], rx_r.at[k, 2], xup)
        flying[k, 3] = send(part.at[k, tokens(-1, 0)], ra2.at[k], rx_s.at[k, 3], rx_r.at[k, 3], xdn)

    def relay(k):
        flying[k, 0].wait_recv()
        ra1[k] = ra1[k] + part[k, tokens(1, 0), :]
        flying[k, 4] = send(ra1.at[k], ra3.at[k], rx_s.at[k, 4], rx_r.at[k, 4], xup)
        flying[k, 1].wait_recv()
        rb1[k] = rb1[k] + part[k, tokens(-1, 1), :]
        flying[k, 5] = send(rb1.at[k], rb3.at[k], rx_s.at[k, 5], rx_r.at[k, 5], xdn)

    def final(k):
        for i in (2, 3, 4, 5):
            flying[k, i].wait_recv()
        logit[pl.ds(k * GT, GH), :] = part[k, tokens(0, 0), :] + ra2[k] + ra3[k]
        logit[pl.ds(k * GT + GH, GH), :] = part[k, tokens(0, 1), :] + rb2[k] + rb3[k]

    swaps = {}

    def exchange(k, src, dst, ssem, rsem, group):
        swaps[k] = [send(src, dst.at[k, i], ssem.at[k, i], rsem.at[k, i], group(i))
                    for i in range(1, 8)]

    def local_stats(k):
        @pl.loop(0, GT // 32)
        def _(i):
            r = pl.ds(pl.multiple_of(i * 32, 32), 32)
            t = logit[pl.ds(pl.multiple_of(k * GT + i * 32, 32), 32), :]
            m = jnp.max(t, axis=1, keepdims=True)
            t = t - m
            w = jnp.where(lane == 0, m, wt[k, r, :])
            w = jnp.where(lane == 1, jnp.sum(jnp.exp(t), axis=1, keepdims=True), w)
            for q in range(NT):
                w = jnp.where(lane == 2 + q, jnp.sum(jnp.exp(t * inv[q]), axis=1, keepdims=True), w)
            wt[k, r, :] = w

        flat = wt[k].T
        st[k, 0] = jnp.where(left, flat[0:8, :], pltpu.roll(flat[8:16, :], 64, 1))
        exchange(k, st.at[k, 0], r1, s1_s, s1_r, group1)

    def merge(k, mine, got):
        for f in swaps[k]:
            f.wait_recv()
        all_s = [st[k, mine]] + [got[k, i] for i in range(1, 8)]
        top = all_s[0][0:1, :]
        for s in all_s[1:]:
            top = jnp.maximum(top, s[0:1, :])
        acc = None
        for s in all_s:
            t = s * jnp.exp((s[0:1, :] - top) * invc)
            acc = t if acc is None else acc + t
        return top, acc

    def merge1(k):
        top, acc = merge(k, 0, r1)
        st[k, 1] = jnp.where(row2 == 0, top, acc)
        exchange(k, st.at[k, 1], r2, s2_s, s2_r, group2)

    base = v * COLS
    col = lax.broadcasted_iota(jnp.int32, (32, CW), 1).astype(F32)

    def grad(k):
        top, acc = merge(k, 1, r2)
        acc = jnp.where(wcol > 0.0, acc, 1.0)
        both = jnp.where(row2 == 0, top, wcol / acc)
        ct[pl.ds(0, 8), :] = both
        ct[pl.ds(8, 8), :] = pltpu.roll(both, 64, 1)
        ct[pl.ds(16, 112), :] = jnp.zeros((112, 128), F32)
        coef[...] = ct[...].T

        for i in range(GT // 32):
            cf = coef[pl.ds(i * 32, 32), :]
            r = pl.ds(k * GT + i * 32, 32)
            lb = lab[r, 0:1]

            @pl.loop(0, NCH)
            def _(j):
                cc = pl.ds(pl.multiple_of(j * CW, CW), CW)
                s = logit[r, cc] - cf[:, 0:1]
                t = teach[r, cc].astype(F32) - cf[:, 8:9]
                g = cf[:, 1:2] * jnp.exp(s)
                g = g - jnp.where(col + (base + j * CW).astype(F32) == lb, mix[0], 0.0)
                for q in range(NT):
                    g = g + cf[:, 2 + q:3 + q] * jnp.exp(s * inv[q])
                    g = g - cf[:, 9 + q:10 + q] * jnp.exp(t * inv[q])
                out = pl.ds(pl.multiple_of(k * CT + x * GT + i * 32, 32), 32)
                grads[out, cc] = g.astype(BF)

        b = grads.at[pl.ds(pl.multiple_of(k * CT + x * GT, GT), GT)]
        flying[k, 6] = send(b, b, gx_s.at[k, 0], gx_r.at[k, 0], xup)
        flying[k, 7] = send(b, b, gx_s.at[k, 1], gx_r.at[k, 1], xdn)

    def passon(k):
        a = grads.at[pl.ds(pl.multiple_of(k * CT + xrel(-1) * GT, GH), GH)]
        b = grads.at[pl.ds(pl.multiple_of(k * CT + xrel(1) * GT + GH, GH), GH)]
        flying[k, 6].wait_recv()
        flying[k, 8] = send(a, a, gx_s.at[k, 2], gx_r.at[k, 2], xup)
        flying[k, 7].wait_recv()
        flying[k, 9] = send(b, b, gx_s.at[k, 3], gx_r.at[k, 3], xdn)

    def landed(k):
        for i in (8, 9):
            flying[k, i].wait_recv()

    pairs = {}

    def pair(k, i):
        yb = yrel(SPREAD[i])
        r = lax.dot_general(hd[:, yb].reshape(512, COLS), grads[pl.ds(k * CT, CT), :],
                            (((1,), (1,)), ((), ())), preferred_element_type=F32)
        tmp[...] = r.reshape(NZ, NC, LROWS, CT)
        hgo[k, i] = tmp[:, c]
        ps[k, i] = tmp[:, 1 - c].astype(BF)
        pairs[k, i] = send(ps.at[k, i], pr.at[k, i], pp_s.at[k, i], pp_r.at[k, i], mate)

    LO, HI = pl.ds(0, LH), pl.ds(LH, LH)

    def total(k, i, part_of):
        return hgo[k, i, :, :, part_of] + pr[k, i, :, :, part_of].astype(F32)

    hops = {}

    def yhop(k, i, val, dev):
        ysb[k, i] = val.astype(BF)
        hops[k, i] = send(ysb.at[k, i], yrb.at[k, i], yy_s.at[k, i], yy_r.at[k, i], dev)

    def scatter(k, step):
        if step == 0:
            pairs[k, 0].wait_recv()
            yhop(k, 0, total(k, 0, LO), yup)
            yhop(k, 1, total(k, 0, HI), ydn)
        elif step == 1:
            pairs[k, 1].wait_recv()
            yhop(k, 2, total(k, 1, HI), yup)
            pairs[k, 2].wait_recv()
            yhop(k, 3, total(k, 2, LO), ydn)
        elif step == 2:
            hops[k, 0].wait_recv()
            yhop(k, 4, total(k, 1, LO) + yrb[k, 0].astype(F32), yup)
            hops[k, 1].wait_recv()
            yhop(k, 5, total(k, 2, HI) + yrb[k, 1].astype(F32), ydn)
        elif step == 3:
            pairs[k, 3].wait_recv()
            for i in (2, 3, 4, 5):
                hops[k, i].wait_recv()
            ysum[:, :, LO] = total(k, 3, LO) + yrb[k, 3].astype(F32) + yrb[k, 4].astype(F32)
            ysum[:, :, HI] = total(k, 3, HI) + yrb[k, 2].astype(F32) + yrb[k, 5].astype(F32)
            zsb[k] = ysum[...].astype(BF)
            res[k] = ysum[z]
            for i in range(1, NZ):
                hops[k, "z", i] = send(zsb.at[k, zrel(i)], zrb.at[k, i],
                                       zz_s.at[k, i], zz_r.at[k, i], group2(i))
        else:
            for i in range(1, NZ):
                hops[k, "z", i].wait_recv()
            acc = res[k]
            for i in range(1, NZ):
                acc = acc + zrb[k, i].astype(F32)
            res[k] = acc

    outs = []

    def head_part(b):
        for j in range(NCH):
            cc = pl.ds(j * CW, CW)
            r = None
            for k in range(K):
                t = jnp.dot(hb[k, b].reshape(256, CT), grads[pl.ds(k * CT, CT), cc],
                            preferred_element_type=F32)
                r = t if r is None else r + t
            hdo[pl.ds(b * 256, 256), cc] = r.astype(BF)
        rows = pl.ds(b * 256, 256)
        outs.append(pltpu.make_async_copy(hdo.at[rows], hdgrad.at[rows], out_sem.at[b]))
        outs[-1].start()

    NEAREST = (1, 7, 2, 6, 3, 5, 4)
    for i in NEAREST:
        zin[0, i].wait_recv()
        piece_out(i)
    give(0, 0)
    zsend(1)
    for i in (0,) + NEAREST:
        piece_on(i)
    give(0, 1)
    give(0, 2)
    zsend(2)
    head_copy.wait()
    stage(0, 0)
    yfirst(1)
    stage(0, 1)
    stage(0, 2)
    for i in (0,) + NEAREST:
        fin[i, 2].wait_recv()
        fin[i, 3].wait_recv()
    give(0, 3)
    stage(0, 3)
    far(0)
    near(0)
    ysecond(1)
    teacher_stats(1)
    stage(1, 0)
    yfirst(2)
    stage(1, 1)
    stage(1, 2)
    ythird(1)
    relay(0)
    stage(1, 3)
    far(1)
    near(1)
    teacher_stats(2)
    ysecond(2)
    stage(2, 0)
    stage(2, 1)
    stage(2, 2)
    ythird(2)
    final(0)
    local_stats(0)
    stage(2, 3)
    far(2)
    relay(1)
    near(2)
    merge1(0)
    relay(2)
    grad(0)
    final(1)
    local_stats(1)
    merge1(1)
    final(2)
    local_stats(2)
    passon(0)
    merge1(2)
    grad(1)
    landed(0)
    pair(0, 0)
    pair(0, 1)
    scatter(0, 0)
    passon(1)
    grad(2)
    pair(0, 2)
    pair(0, 3)
    scatter(0, 1)
    scatter(0, 2)
    landed(1)
    pair(1, 0)
    pair(1, 1)
    scatter(1, 0)
    passon(2)
    scatter(0, 3)
    pair(1, 2)
    pair(1, 3)
    scatter(1, 1)
    landed(2)
    pair(2, 0)
    scatter(1, 2)
    pair(2, 1)
    pair(2, 2)
    scatter(2, 0)
    pair(2, 3)
    scatter(1, 3)
    scatter(2, 1)
    head_part(0)
    head_part(1)
    scatter(2, 2)
    head_part(2)
    head_part(3)
    head_part(4)
    scatter(2, 3)
    for b in (5, 6, 7):
        head_part(b)
    scatter(0, 4)
    scatter(1, 4)
    scatter(2, 4)

    full = [res[k] for k in range(K)]
    hgrad[...] = jnp.concatenate(
        [full[k][:, d * GT:(d + 1) * GT] for d in range(NX) for k in range(K)], axis=1)

    for cp in sent:
        cp.wait_send()
    for cp in outs:
        cp.wait()


def shards(hidden_t, head, teacher, labels, temps, mix):
    vmem = pl.BlockSpec(memory_space=pltpu.VMEM)
    hbm = pl.BlockSpec(memory_space=pl.ANY)
    dma = pltpu.SemaphoreType.DMA
    half = (K, GH, COLS)
    return pl.pallas_call(
        body,
        out_shape=(
            pltpu.VMEM((LROWS, TOK), F32),
            pltpu.VMEM((FEAT, COLS), BF),
        ),
        in_specs=[hbm] * 6,
        out_specs=(vmem, hbm),
        scratch_shapes=[
            pltpu.VMEM((LROWS, TOK), BF),
            pltpu.VMEM((1, OWN), jnp.int32),
            pltpu.SMEM((NT,), F32),
            pltpu.SMEM((2,), F32),
            pltpu.VMEM((FEAT, COLS), BF),
            pltpu.VMEM((K, NZ, NY, NC, LROWS, CT), BF),
            pltpu.VMEM((NZ, NY, NC * LROWS, COLS), BF),
            pltpu.VMEM((CT, 512), BF),
            pltpu.VMEM((K, CT, COLS), F32),
            pltpu.VMEM(half, F32), pltpu.VMEM(half, F32),
            pltpu.VMEM(half, F32), pltpu.VMEM(half, F32),
            pltpu.VMEM(half, F32), pltpu.VMEM(half, F32),
            pltpu.VMEM((OWN, COLS), F32),
            pltpu.VMEM((OWN, COLS), BF),
            pltpu.VMEM((K, 128, 128), F32),
            pltpu.VMEM((K, 2, 8, 128), F32),
            pltpu.VMEM((K, 8, 8, 128), F32),
            pltpu.VMEM((K, 8, 8, 128), F32),
            pltpu.VMEM((128, 128), F32),
            pltpu.VMEM((128, 128), F32),
            pltpu.VMEM((256, 128), F32),
            pltpu.VMEM((TOK, COLS), BF),
            pltpu.VMEM((NZ, NC, LROWS, CT), F32),
            pltpu.VMEM((K, NY, NZ, LROWS, CT), F32),
            pltpu.VMEM((K, NY, NZ, LROWS, CT), BF),
            pltpu.VMEM((K, NY, NZ, LROWS, CT), BF),
            pltpu.VMEM((K, 6, NZ, LROWS, LH), BF),
            pltpu.VMEM((K, 6, NZ, LROWS, LH), BF),
            pltpu.VMEM((NZ, LROWS, CT), F32),
            pltpu.VMEM((K, NZ, LROWS, CT), BF),
            pltpu.VMEM((K, NZ, LROWS, CT), BF),
            pltpu.VMEM((K, LROWS, CT), F32),
            dma((6,)), dma((8,)),
            dma((NZ, 4)), dma((NZ, 4)),
            dma((K, 4)), dma((K, 4)),
            dma((K, NZ)), dma((K, NZ)),
            dma((K, 4)), dma((K, 4)),
            dma((K, 6)), dma((K, 6)),
            dma((K, 8)), dma((K, 8)),
            dma((K, 8)), dma((K, 8)),
            dma((K, 4)), dma((K, 4)),
            dma((K, 4)), dma((K, 4)),
            dma((K, 8)), dma((K, 8)),
            dma((K, 6)), dma((K, 6)),
        ],
        compiler_params=pltpu.CompilerParams(
            collective_id=0, has_side_effects=True, vmem_limit_bytes=56 * 1024 * 1024
        ),
    )(hidden_t, head.reshape(NZ, NY, NC * LROWS, COLS), teacher, labels.reshape(1, OWN), temps, mix)


def solution(mesh):
    placed = (P(("dp", "vocab"), None), P("dp", "vocab"), P("dp", "vocab"), P("dp"), P(), P())
    return jax.shard_map(
        shards,
        mesh=mesh,
        in_specs=placed,
        out_specs=(P(("dp", "vocab"), None), P("dp", "vocab")),
        check_vma=False,
    )
```

```python
import jax
import jax.numpy as jnp
from jax import lax
from jax.experimental import pallas as pl
from jax.experimental.pallas import tpu as pltpu
from jax.sharding import PartitionSpec as P

BF = jnp.bfloat16
F32 = jnp.float32
MESH = pl.DeviceIdType.MESH
NX, NZ, NY, NC = 4, 8, 4, 2
TOK, OWN = 768, 192
K = 3
CT = TOK // K
GT = CT // NX
GH = GT // 2
LH = CT // 2
COLS, CW, NCH = 1280, 256, 5
FEAT, LROWS = 2048, 32
NT = 4
GATHER = (0, -1, 1, 2)
SPREAD = (2, 1, -1, 0)


def body(hid_hbm, head_hbm, teach_hbm, labels_hbm, temps_hbm, mix_hbm,
         hgrad, hdgrad,
         hid, labels, temps, mix,
         hb, hd, ht, part, ra1, rb1, rr, logit, teach,
         wt, st, r1, r2, ct, coef, lab, grads, tmp, hgo, ps, pr, ysb, yrb, ysum, zsb, zrb, res,
         loc_sem, fy_s, fy_r, fq_r, ay_s, ay_r, az_s, az_r, ap_s, ap_r,
         rx_s, rx_r, s1_s, s1_r, s2_s, s2_r, gx_s, gx_r,
         pp_s, pp_r, zz_s, zz_r, yy_s, yy_r):
    x = lax.axis_index("dp")
    v = lax.axis_index("vocab")
    c = lax.rem(v, 2)
    y = lax.rem(v // 2, NY)
    z = v // (NY * NC)

    def vid(zz, yy, cc):
        return {"vocab": (zz * NY + yy) * NC + cc}

    def zrel(d):
        return lax.rem(z + (d + NZ), NZ)

    def yrel(d):
        return lax.rem(y + (d + NY), NY)

    def xrel(d):
        return lax.rem(x + (d + NX), NX)

    yup, ydn = vid(z, yrel(1), c), vid(z, yrel(-1), c)
    mate = vid(z, y, 1 - c)
    xup, xdn = {"dp": xrel(1)}, {"dp": xrel(-1)}
    slot = y * NC + c

    def group1(k):
        other = lax.rem(slot + k, 8)
        return vid(z, other // NC, lax.rem(other, NC))

    def group2(k):
        return vid(zrel(k), y, c)

    def send(src, dst, ssem, rsem, dev):
        cp = pltpu.make_async_remote_copy(
            src_ref=src, dst_ref=dst, send_sem=ssem, recv_sem=rsem,
            device_id=dev, device_id_type=MESH)
        cp.start()
        return cp

    def all_in(ref, sem):
        pltpu.make_async_remote_copy(
            src_ref=ref, dst_ref=ref, send_sem=sem, recv_sem=sem,
            device_id=mate, device_id_type=MESH).wait_recv()

    def all_out(ref, sem):
        pltpu.make_async_remote_copy(
            src_ref=ref, dst_ref=ref, send_sem=sem, recv_sem=sem,
            device_id=mate, device_id_type=MESH).wait_send()

    small = []
    for n, (a, b) in enumerate(((hid_hbm, hid), (labels_hbm, labels), (temps_hbm, temps), (mix_hbm, mix))):
        cp = pltpu.make_async_copy(a, b, loc_sem.at[2 + n])
        cp.start()
        small.append(cp)

    bar = pltpu.get_barrier_semaphore()
    for k in range(4, 0, -1):
        for i in {4: (4,)}.get(k, (k, NZ - k)):
            pl.semaphore_signal(bar, inc=1, device_id=group2(i), device_id_type=MESH)
    for k in range(1, 8):
        pl.semaphore_signal(bar, inc=1, device_id=group1(k), device_id_type=MESH)
    pl.semaphore_signal(bar, inc=1, device_id=xup, device_id_type=MESH)
    pl.semaphore_signal(bar, inc=1, device_id=xdn, device_id_type=MESH)

    head_copy = pltpu.make_async_copy(head_hbm, hd, loc_sem.at[0])
    head_copy.start()
    teach_copy = pltpu.make_async_copy(teach_hbm, teach, loc_sem.at[1])
    teach_copy.start()

    for cp in small:
        cp.wait()

    h32 = hid[...].astype(F32)
    for k in range(K):
        piece = jnp.concatenate(
            [h32[:, d * OWN + k * GT:d * OWN + (k + 1) * GT] for d in range(NX)], axis=1)
        hb[k, z, y, c] = piece.astype(BF)

    pl.semaphore_wait(bar, 16)

    zin = {}
    fin = {}

    def zsend(k):
        own = hb.at[k, z, y, c]
        for i in range(1, NZ):
            zin[k, i] = send(own, own, az_s.at[k], az_r.at[i - 1 if k == 0 else 6 + k], group2(i))

    def piece_out(i):
        b = hb.at[0, zrel(-i), y, c]
        fin[i, 0] = send(b, b, fy_s.at[0], fy_r.at[i, 0], yup)
        fin[i, 1] = send(b, b, fy_s.at[1], fy_r.at[i, 1], ydn)

    def piece_on(i):
        fin[i, 0].wait_recv()
        b = hb.at[0, zrel(-i), yrel(-1), c, :, pl.ds(0, LH)]
        send(b, b, fy_s.at[2], fq_r.at[0], yup)
        fin[i, 1].wait_recv()
        b = hb.at[0, zrel(-i), yrel(1), c, :, pl.ds(LH, LH)]
        send(b, b, fy_s.at[3], fq_r.at[1], ydn)

    zsend(0)
    piece_out(0)

    inv = [1.0 / temps[q] for q in range(NT)]
    lane = lax.broadcasted_iota(jnp.int32, (32, 128), 1)
    row2 = lax.broadcasted_iota(jnp.int32, (8, 128), 0)
    left = lax.broadcasted_iota(jnp.int32, (8, 128), 1) < 64
    invc = jnp.where(left & (row2 == 1), 1.0, 0.0)
    wcol = jnp.where(left & (row2 == 1), mix[0], 0.0)
    for q in range(NT):
        hit = (left & (row2 == 2 + q)) | (jnp.logical_not(left) & (row2 == 1 + q))
        invc = jnp.where(hit, inv[q], invc)
        wcol = jnp.where(hit, mix[1] * temps[q], wcol)

    lab[...] = jnp.zeros((256, 128), F32)
    labrow = jnp.concatenate(
        [labels[...].astype(F32), jnp.zeros((1, 256 - OWN), F32)], axis=1)
    lab[...] = jnp.broadcast_to(labrow, (128, 256)).T

    teach_copy.wait()

    def teacher_stats(k):
        @pl.loop(0, GT // 32)
        def _(i):
            r = pl.ds(pl.multiple_of(i * 32, 32), 32)
            t = teach[pl.ds(pl.multiple_of(k * GT + i * 32, 32), 32), :].astype(F32)
            m = jnp.max(t, axis=1, keepdims=True)
            t = t - m
            w = jnp.where(lane == 8, m, 0.0)
            for q in range(NT):
                w = jnp.where(lane == 9 + q, jnp.sum(jnp.exp(t * inv[q]), axis=1, keepdims=True), w)
            wt[k, r, :] = w

        wt[k, pl.ds(GT, 128 - GT), :] = jnp.zeros((128 - GT, 128), F32)

    teacher_stats(0)

    yin = {}
    gives = {}

    def bundle(k, d):
        return hb.at[k, :, yrel(d), c]

    def give(k, i):
        b = bundle(k, GATHER[i])
        gives[k, i] = send(b, b, ap_s.at[k], ap_r.at[k, i], mate)

    def yfirst(k):
        all_in(hb.at[k, pl.ds(0, NZ - 1), y, c], az_r.at[6 + k])
        b = bundle(k, 0)
        yin[k, 0] = send(b, b, ay_s.at[k - 1], ay_r.at[k - 1, 0], yup)
        yin[k, 1] = send(b, b, ay_s.at[k - 1], ay_r.at[k - 1, 1], ydn)
        give(k, 0)

    def ysecond(k):
        yin[k, 0].wait_recv()
        b = hb.at[k, :, yrel(-1), c, :, pl.ds(0, LH)]
        send(b, b, ay_s.at[k - 1], ay_r.at[k - 1, 2], yup)
        yin[k, 1].wait_recv()
        b = hb.at[k, :, yrel(1), c, :, pl.ds(LH, LH)]
        send(b, b, ay_s.at[k - 1], ay_r.at[k - 1, 2], ydn)
        give(k, 1)
        give(k, 2)

    def ythird(k):
        all_in(hb.at[k, :, yrel(2), c], ay_r.at[k - 1, 2])
        give(k, 3)

    def stage(k, i):
        gives[k, i].wait_recv()
        yb = yrel(GATHER[i])
        ht[...] = hb[k, :, yb].reshape(512, CT).T

        for j in range(NCH):
            cc = pl.ds(j * CW, CW)
            acc = jnp.dot(ht[...], hd[:, yb, :, cc].reshape(512, CW), preferred_element_type=F32)
            if i != 0:
                acc = acc + part[k, :, cc]
            part[k, :, cc] = acc

    def tokens(d, half):
        return pl.ds(pl.multiple_of(xrel(d) * GT + half * GH, GH), GH)

    flying = {}

    def far(k):
        flying[k, 0] = send(part.at[k, tokens(2, 0)], ra1.at[k], rx_s.at[k], rx_r.at[k, 0], xup)
        flying[k, 1] = send(part.at[k, tokens(2, 1)], rb1.at[k], rx_s.at[k], rx_r.at[k, 1], xdn)

    def near(k):
        send(part.at[k, tokens(1, 1)], rr.at[k, 0], rx_s.at[k], rx_r.at[k, 2], xup)
        send(part.at[k, tokens(-1, 0)], rr.at[k, 1], rx_s.at[k], rx_r.at[k, 2], xdn)

    def relay(k):
        flying[k, 0].wait_recv()
        ra1[k] = ra1[k] + part[k, tokens(1, 0), :]
        send(ra1.at[k], rr.at[k, 2], rx_s.at[k], rx_r.at[k, 2], xup)
        flying[k, 1].wait_recv()
        rb1[k] = rb1[k] + part[k, tokens(-1, 1), :]
        send(rb1.at[k], rr.at[k, 3], rx_s.at[k], rx_r.at[k, 2], xdn)

    def final(k):
        all_in(rr.at[k], rx_r.at[k, 2])
        logit[pl.ds(k * GT, GH), :] = part[k, tokens(0, 0), :] + rr[k, 1] + rr[k, 2]
        logit[pl.ds(k * GT + GH, GH), :] = part[k, tokens(0, 1), :] + rr[k, 0] + rr[k, 3]

    def exchange(k, src, dst, ssem, rsem, group):
        for i in range(1, 8):
            send(src, dst.at[k, i], ssem.at[k], rsem.at[k], group(i))

    def local_stats(k):
        @pl.loop(0, GT // 32)
        def _(i):
            r = pl.ds(pl.multiple_of(i * 32, 32), 32)
            t = logit[pl.ds(pl.multiple_of(k * GT + i * 32, 32), 32), :]
            m = jnp.max(t, axis=1, keepdims=True)
            t = t - m
            w = jnp.where(lane == 0, m, wt[k, r, :])
            w = jnp.where(lane == 1, jnp.sum(jnp.exp(t), axis=1, keepdims=True), w)
            for q in range(NT):
                w = jnp.where(lane == 2 + q, jnp.sum(jnp.exp(t * inv[q]), axis=1, keepdims=True), w)
            wt[k, r, :] = w

        flat = wt[k].T
        st[k, 0] = jnp.where(left, flat[0:8, :], pltpu.roll(flat[8:16, :], 64, 1))
        exchange(k, st.at[k, 0], r1, s1_s, s1_r, group1)

    def merge(k, mine, got, rsem):
        all_in(got.at[k, pl.ds(1, 7)], rsem.at[k])
        all_s = [st[k, mine]] + [got[k, i] for i in range(1, 8)]
        top = all_s[0][0:1, :]
        for s in all_s[1:]:
            top = jnp.maximum(top, s[0:1, :])
        acc = None
        for s in all_s:
            t = s * jnp.exp((s[0:1, :] - top) * invc)
            acc = t if acc is None else acc + t
        return top, acc

    def merge1(k):
        top, acc = merge(k, 0, r1, s1_r)
        st[k, 1] = jnp.where(row2 == 0, top, acc)
        exchange(k, st.at[k, 1], r2, s2_s, s2_r, group2)

    base = v * COLS
    col = lax.broadcasted_iota(jnp.int32, (32, CW), 1).astype(F32)

    def grad(k):
        top, acc = merge(k, 1, r2, s2_r)
        acc = jnp.where(wcol > 0.0, acc, 1.0)
        both = jnp.where(row2 == 0, top, wcol / acc)
        ct[pl.ds(0, 8), :] = both
        ct[pl.ds(8, 8), :] = pltpu.roll(both, 64, 1)
        ct[pl.ds(16, 112), :] = jnp.zeros((112, 128), F32)
        coef[...] = ct[...].T

        for i in range(GT // 32):
            cf = coef[pl.ds(i * 32, 32), :]
            r = pl.ds(k * GT + i * 32, 32)
            lb = lab[r, 0:1]

            @pl.loop(0, NCH)
            def _(j):
                cc = pl.ds(pl.multiple_of(j * CW, CW), CW)
                s = logit[r, cc] - cf[:, 0:1]
                t = teach[r, cc].astype(F32) - cf[:, 8:9]
                g = cf[:, 1:2] * jnp.exp(s)
                g = g - jnp.where(col + (base + j * CW).astype(F32) == lb, mix[0], 0.0)
                for q in range(NT):
                    g = g + cf[:, 2 + q:3 + q] * jnp.exp(s * inv[q])
                    g = g - cf[:, 9 + q:10 + q] * jnp.exp(t * inv[q])
                out = pl.ds(pl.multiple_of(k * CT + x * GT + i * 32, 32), 32)
                grads[out, cc] = g.astype(BF)

        b = grads.at[pl.ds(pl.multiple_of(k * CT + x * GT, GT), GT)]
        flying[k, 6] = send(b, b, gx_s.at[k], gx_r.at[k, 0], xup)
        flying[k, 7] = send(b, b, gx_s.at[k], gx_r.at[k, 1], xdn)

    def passon(k):
        a = grads.at[pl.ds(pl.multiple_of(k * CT + xrel(-1) * GT, GH), GH)]
        b = grads.at[pl.ds(pl.multiple_of(k * CT + xrel(1) * GT + GH, GH), GH)]
        flying[k, 6].wait_recv()
        send(a, a, gx_s.at[k], gx_r.at[k, 2], xup)
        flying[k, 7].wait_recv()
        send(b, b, gx_s.at[k], gx_r.at[k, 2], xdn)

    def landed(k):
        all_in(grads.at[pl.ds(pl.multiple_of(k * CT + xrel(2) * GT, GT), GT)], gx_r.at[k, 2])

    pairs = {}

    def pair(k, i):
        yb = yrel(SPREAD[i])
        r = lax.dot_general(hd[:, yb].reshape(512, COLS), grads[pl.ds(k * CT, CT), :],
                            (((1,), (1,)), ((), ())), preferred_element_type=F32)
        tmp[...] = r.reshape(NZ, NC, LROWS, CT)
        hgo[k, i] = tmp[:, c]
        ps[k, i] = tmp[:, 1 - c].astype(BF)
        pairs[k, i] = send(ps.at[k, i], pr.at[k, i], pp_s.at[k], pp_r.at[k, i], mate)

    LO, HI = pl.ds(0, LH), pl.ds(LH, LH)

    def total(k, i, part_of):
        return hgo[k, i, :, :, part_of] + pr[k, i, :, :, part_of].astype(F32)

    hops = {}

    def yhop(k, i, val, dev):
        ysb[k, i] = val.astype(BF)
        hops[k, i] = send(ysb.at[k, i], yrb.at[k, i], yy_s.at[k], yy_r.at[k, min(i, 2)], dev)

    def scatter(k, step):
        if step == 0:
            pairs[k, 0].wait_recv()
            yhop(k, 0, total(k, 0, LO), yup)
            yhop(k, 1, total(k, 0, HI), ydn)
        elif step == 1:
            pairs[k, 1].wait_recv()
            yhop(k, 2, total(k, 1, HI), yup)
            pairs[k, 2].wait_recv()
            yhop(k, 3, total(k, 2, LO), ydn)
        elif step == 2:
            hops[k, 0].wait_recv()
            yhop(k, 4, total(k, 1, LO) + yrb[k, 0].astype(F32), yup)
            hops[k, 1].wait_recv()
            yhop(k, 5, total(k, 2, HI) + yrb[k, 1].astype(F32), ydn)
        elif step == 3:
            pairs[k, 3].wait_recv()
            all_in(yrb.at[k, pl.ds(2, 4)], yy_r.at[k, 2])
            ysum[:, :, LO] = total(k, 3, LO) + yrb[k, 3].astype(F32) + yrb[k, 4].astype(F32)
            ysum[:, :, HI] = total(k, 3, HI) + yrb[k, 2].astype(F32) + yrb[k, 5].astype(F32)
            zsb[k] = ysum[...].astype(BF)
            res[k] = ysum[z]
            for i in range(1, NZ):
                send(zsb.at[k, zrel(i)], zrb.at[k, i], zz_s.at[k], zz_r.at[k], group2(i))
        else:
            all_in(zrb.at[k, pl.ds(1, NZ - 1)], zz_r.at[k])
            acc = res[k]
            for i in range(1, NZ):
                acc = acc + zrb[k, i].astype(F32)
            res[k] = acc

    def head_part(b):
        for j in range(NCH):
            cc = pl.ds(j * CW, CW)
            r = None
            for k in range(K):
                t = jnp.dot(hb[k, b].reshape(256, CT), grads[pl.ds(k * CT, CT), cc],
                            preferred_element_type=F32)
                r = t if r is None else r + t
            hdgrad[pl.ds(b * 256, 256), cc] = r.astype(BF)

    NEAREST = (1, 7, 2, 6, 3, 5, 4)
    for i in NEAREST:
        zin[0, i].wait_recv()
        piece_out(i)
        if i == 7:
            zsend(1)
    give(0, 0)
    zsend(2)
    for i in (0,) + NEAREST:
        piece_on(i)
    give(0, 1)
    give(0, 2)
    head_copy.wait()
    stage(0, 0)
    yfirst(1)
    stage(0, 1)
    stage(0, 2)
    far_y = hb.at[0, :, yrel(2), c]
    all_in(far_y.at[:, :, pl.ds(0, LH)], fq_r.at[0])
    all_in(far_y.at[:, :, pl.ds(LH, LH)], fq_r.at[1])
    give(0, 3)
    stage(0, 3)
    far(0)
    near(0)
    ysecond(1)
    teacher_stats(1)
    stage(1, 0)
    yfirst(2)
    stage(1, 1)
    stage(1, 2)
    relay(0)
    ythird(1)
    stage(1, 3)
    far(1)
    near(1)
    teacher_stats(2)
    ysecond(2)
    stage(2, 0)
    stage(2, 1)
    stage(2, 2)
    ythird(2)
    final(0)
    local_stats(0)
    stage(2, 3)
    far(2)
    relay(1)
    near(2)
    merge1(0)
    relay(2)
    grad(0)
    final(1)
    local_stats(1)
    merge1(1)
    final(2)
    local_stats(2)
    passon(0)
    grad(1)
    merge1(2)
    landed(0)
    pair(0, 0)
    pair(0, 1)
    scatter(0, 0)
    passon(1)
    grad(2)
    pair(0, 2)
    pair(0, 3)
    scatter(0, 1)
    scatter(0, 2)
    landed(1)
    pair(1, 0)
    pair(1, 1)
    scatter(1, 0)
    passon(2)
    pair(1, 2)
    pair(1, 3)
    scatter(1, 1)
    landed(2)
    pair(2, 0)
    scatter(0, 3)
    scatter(1, 2)
    pair(2, 1)
    pair(2, 2)
    scatter(2, 0)
    pair(2, 3)
    scatter(2, 1)
    head_part(0)
    head_part(1)
    head_part(2)
    scatter(2, 2)
    scatter(1, 3)
    head_part(3)
    head_part(4)
    head_part(5)
    scatter(2, 3)
    for b in (6, 7):
        head_part(b)
    scatter(0, 4)
    scatter(1, 4)
    scatter(2, 4)

    full = [res[k] for k in range(K)]
    hgrad[...] = jnp.concatenate(
        [full[k][:, d * GT:(d + 1) * GT] for d in range(NX) for k in range(K)], axis=1)

    one = hb.at[0, :, y, c]
    for i in (0, 1):
        all_out(one, fy_s.at[i])
        all_out(one.at[:, :, pl.ds(0, LH)], fy_s.at[2 + i])
    for k in range(K):
        all_out(hb.at[k, pl.ds(0, NZ - 1), y, c], az_s.at[k])
        all_out(hb.at[k, :, :, c], ap_s.at[k])
        if k > 0:
            all_out(hb.at[k, :, pl.ds(0, 3), c], ay_s.at[k - 1])
        all_out(logit, rx_s.at[k])
        all_out(r1.at[k, pl.ds(1, 7)], s1_s.at[k])
        all_out(r2.at[k, pl.ds(1, 7)], s2_s.at[k])
        all_out(grads.at[pl.ds(0, OWN)], gx_s.at[k])
        all_out(ps.at[k], pp_s.at[k])
        all_out(ysb.at[k], yy_s.at[k])
        all_out(zrb.at[k, pl.ds(1, NZ - 1)], zz_s.at[k])


def shards(hidden_t, head, teacher, labels, temps, mix):
    vmem = pl.BlockSpec(memory_space=pltpu.VMEM)
    hbm = pl.BlockSpec(memory_space=pl.ANY)
    dma = pltpu.SemaphoreType.DMA
    half = (K, GH, COLS)
    return pl.pallas_call(
        body,
        out_shape=(
            pltpu.VMEM((LROWS, TOK), F32),
            pltpu.VMEM((FEAT, COLS), BF),
        ),
        in_specs=[hbm] * 6,
        out_specs=(vmem, vmem),
        scratch_shapes=[
            pltpu.VMEM((LROWS, TOK), BF),
            pltpu.VMEM((1, OWN), jnp.int32),
            pltpu.SMEM((NT,), F32),
            pltpu.SMEM((2,), F32),
            pltpu.VMEM((K, NZ, NY, NC, LROWS, CT), BF),
            pltpu.VMEM((NZ, NY, NC * LROWS, COLS), BF),
            pltpu.VMEM((CT, 512), BF),
            pltpu.VMEM((K, CT, COLS), F32),
            pltpu.VMEM(half, F32), pltpu.VMEM(half, F32),
            pltpu.VMEM((K, 4, GH, COLS), F32),
            pltpu.VMEM((OWN, COLS), F32),
            pltpu.VMEM((OWN, COLS), BF),
            pltpu.VMEM((K, 128, 128), F32),
            pltpu.VMEM((K, 2, 8, 128), F32),
            pltpu.VMEM((K, 8, 8, 128), F32),
            pltpu.VMEM((K, 8, 8, 128), F32),
            pltpu.VMEM((128, 128), F32),
            pltpu.VMEM((128, 128), F32),
            pltpu.VMEM((256, 128), F32),
            pltpu.VMEM((TOK, COLS), BF),
            pltpu.VMEM((NZ, NC, LROWS, CT), F32),
            pltpu.VMEM((K, NY, NZ, LROWS, CT), F32),
            pltpu.VMEM((K, NY, NZ, LROWS, CT), BF),
            pltpu.VMEM((K, NY, NZ, LROWS, CT), BF),
            pltpu.VMEM((K, 6, NZ, LROWS, LH), BF),
            pltpu.VMEM((K, 6, NZ, LROWS, LH), BF),
            pltpu.VMEM((NZ, LROWS, CT), F32),
            pltpu.VMEM((K, NZ, LROWS, CT), BF),
            pltpu.VMEM((K, NZ, LROWS, CT), BF),
            pltpu.VMEM((K, LROWS, CT), F32),
            dma((6,)),
            dma((4,)), dma((NZ, 2)), dma((2,)),
            dma((K - 1,)), dma((K - 1, 3)),
            dma((K,)), dma((6 + K,)),
            dma((K,)), dma((K, 4)),
            dma((K,)), dma((K, 3)),
            dma((K,)), dma((K,)),
            dma((K,)), dma((K,)),
            dma((K,)), dma((K, 3)),
            dma((K,)), dma((K, 4)),
            dma((K,)), dma((K,)),
            dma((K,)), dma((K, 3)),
        ],
        compiler_params=pltpu.CompilerParams(
            collective_id=0, has_side_effects=True, vmem_limit_bytes=56 * 1024 * 1024
        ),
    )(hidden_t, head.reshape(NZ, NY, NC * LROWS, COLS), teacher, labels.reshape(1, OWN), temps, mix)


def solution(mesh):
    placed = (P(("dp", "vocab"), None), P("dp", "vocab"), P("dp", "vocab"), P("dp"), P(), P())
    return jax.shard_map(
        shards,
        mesh=mesh,
        in_specs=placed,
        out_specs=(P(("dp", "vocab"), None), P("dp", "vocab")),
        check_vma=False,
    )
```

```python
import jax
import jax.numpy as jnp
from jax import lax
from jax.experimental import pallas as pl
from jax.experimental.pallas import tpu as pltpu
from jax.sharding import PartitionSpec as P

BF = jnp.bfloat16
F32 = jnp.float32
MESH = pl.DeviceIdType.MESH
NX, NZ, NY, NC = 4, 8, 4, 2
TOK, OWN = 768, 192
K = 3
CT = TOK // K
GT = CT // NX
GH = GT // 2
LH = CT // 2
COLS, CW, NCH = 1280, 256, 5
FEAT, LROWS = 2048, 32
NT = 4
GATHER = (0, -1, 1, 2)
SPREAD = (2, 1, -1, 0)
FARTHEST = (4, 3, 5, 2, 6, 1, 7)
PARTS = (((0, 5),), ((0, 5),), ((0, 3), (3, 5)))


def body(hid_hbm, head_hbm, teach_hbm, labels_hbm, temps_hbm, mix_hbm,
         hgrad, hdgrad,
         hid, labels, temps, mix,
         hb, hd, ht, part, ra1, rb1, rr, logit, teach,
         wt, st, r1, r2, ct, coef, lab, grads, tmp, hgo, ps, pr, ysb, yrb, ysum, zsb, zrb, res,
         loc_sem, fy_s, fy_r, fq_r, ay_s, ay_r, az_s, az_r, ap_s, ap_r,
         rx_s, rx_r, s1_s, s1_r, s2_s, s2_r, gx_s, gx_r,
         pp_s, pp_r, zz_s, zz_r, yy_s, yy_r):
    x = lax.axis_index("dp")
    v = lax.axis_index("vocab")
    c = lax.rem(v, 2)
    y = lax.rem(v // 2, NY)
    z = v // (NY * NC)

    def vid(zz, yy, cc):
        return {"vocab": (zz * NY + yy) * NC + cc}

    def zrel(d):
        return lax.rem(z + (d + NZ), NZ)

    def yrel(d):
        return lax.rem(y + (d + NY), NY)

    def xrel(d):
        return lax.rem(x + (d + NX), NX)

    yup, ydn = vid(z, yrel(1), c), vid(z, yrel(-1), c)
    mate = vid(z, y, 1 - c)
    xup, xdn = {"dp": xrel(1)}, {"dp": xrel(-1)}
    slot = y * NC + c

    def group1(k):
        other = lax.rem(slot + k, 8)
        return vid(z, other // NC, lax.rem(other, NC))

    def group2(k):
        return vid(zrel(k), y, c)

    def send(src, dst, ssem, rsem, dev):
        cp = pltpu.make_async_remote_copy(
            src_ref=src, dst_ref=dst, send_sem=ssem, recv_sem=rsem,
            device_id=dev, device_id_type=MESH)
        cp.start()
        return cp

    def all_in(ref, sem):
        pltpu.make_async_remote_copy(
            src_ref=ref, dst_ref=ref, send_sem=sem, recv_sem=sem,
            device_id=mate, device_id_type=MESH).wait_recv()

    def all_out(ref, sem):
        pltpu.make_async_remote_copy(
            src_ref=ref, dst_ref=ref, send_sem=sem, recv_sem=sem,
            device_id=mate, device_id_type=MESH).wait_send()

    small = []
    for n, (a, b) in enumerate(((hid_hbm, hid), (labels_hbm, labels), (temps_hbm, temps), (mix_hbm, mix))):
        cp = pltpu.make_async_copy(a, b, loc_sem.at[2 + n])
        cp.start()
        small.append(cp)

    bar = pltpu.get_barrier_semaphore()
    for k in range(4, 0, -1):
        for i in {4: (4,)}.get(k, (k, NZ - k)):
            pl.semaphore_signal(bar, inc=1, device_id=group2(i), device_id_type=MESH)
    for k in range(1, 8):
        pl.semaphore_signal(bar, inc=1, device_id=group1(k), device_id_type=MESH)
    pl.semaphore_signal(bar, inc=1, device_id=xup, device_id_type=MESH)
    pl.semaphore_signal(bar, inc=1, device_id=xdn, device_id_type=MESH)

    head_copy = pltpu.make_async_copy(head_hbm, hd, loc_sem.at[0])
    head_copy.start()
    teach_copy = pltpu.make_async_copy(teach_hbm, teach, loc_sem.at[1])
    teach_copy.start()

    for cp in small:
        cp.wait()

    h32 = hid[...].astype(F32)
    for k in range(K):
        piece = jnp.concatenate(
            [h32[:, d * OWN + k * GT:d * OWN + (k + 1) * GT] for d in range(NX)], axis=1)
        hb[k, z, y, c] = piece.astype(BF)

    pl.semaphore_wait(bar, 16)

    zin = {}
    fin = {}

    def zsend(k):
        own = hb.at[k, z, y, c]
        for i in FARTHEST:
            zin[k, i] = send(own, own, az_s.at[k], az_r.at[i - 1 if k == 0 else 6 + k], group2(i))

    def piece_out(i):
        b = hb.at[0, zrel(-i), y, c]
        fin[i, 0] = send(b, b, fy_s.at[0], fy_r.at[i, 0], yup)
        fin[i, 1] = send(b, b, fy_s.at[1], fy_r.at[i, 1], ydn)

    def piece_on(i):
        fin[i, 0].wait_recv()
        b = hb.at[0, zrel(-i), yrel(-1), c, :, pl.ds(0, LH)]
        send(b, b, fy_s.at[2], fq_r.at[0], yup)
        fin[i, 1].wait_recv()
        b = hb.at[0, zrel(-i), yrel(1), c, :, pl.ds(LH, LH)]
        send(b, b, fy_s.at[3], fq_r.at[1], ydn)

    zsend(0)
    piece_out(0)

    inv = [1.0 / temps[q] for q in range(NT)]
    lane = lax.broadcasted_iota(jnp.int32, (32, 128), 1)
    row2 = lax.broadcasted_iota(jnp.int32, (8, 128), 0)
    left = lax.broadcasted_iota(jnp.int32, (8, 128), 1) < 64
    invc = jnp.where(left & (row2 == 1), 1.0, 0.0)
    wcol = jnp.where(left & (row2 == 1), mix[0], 0.0)
    for q in range(NT):
        hit = (left & (row2 == 2 + q)) | (jnp.logical_not(left) & (row2 == 1 + q))
        invc = jnp.where(hit, inv[q], invc)
        wcol = jnp.where(hit, mix[1] * temps[q], wcol)

    lab[...] = jnp.zeros((256, 128), F32)
    labrow = jnp.concatenate(
        [labels[...].astype(F32), jnp.zeros((1, 256 - OWN), F32)], axis=1)
    lab[...] = jnp.broadcast_to(labrow, (128, 256)).T

    teach_copy.wait()

    def teacher_stats(k):
        @pl.loop(0, GT // 32)
        def _(i):
            r = pl.ds(pl.multiple_of(i * 32, 32), 32)
            t = teach[pl.ds(pl.multiple_of(k * GT + i * 32, 32), 32), :].astype(F32)
            m = jnp.max(t, axis=1, keepdims=True)
            t = t - m
            w = jnp.where(lane == 8, m, 0.0)
            for q in range(NT):
                w = jnp.where(lane == 9 + q, jnp.sum(jnp.exp(t * inv[q]), axis=1, keepdims=True), w)
            wt[k, r, :] = w

        wt[k, pl.ds(GT, 128 - GT), :] = jnp.zeros((128 - GT, 128), F32)

    teacher_stats(0)

    yin = {}
    gives = {}

    def bundle(k, d):
        return hb.at[k, :, yrel(d), c]

    def give(k, i):
        b = bundle(k, GATHER[i])
        gives[k, i] = send(b, b, ap_s.at[k], ap_r.at[k, i], mate)

    def yfirst(k):
        all_in(hb.at[k, pl.ds(0, NZ - 1), y, c], az_r.at[6 + k])
        b = bundle(k, 0)
        yin[k, 0] = send(b, b, ay_s.at[k - 1], ay_r.at[k - 1, 0], yup)
        yin[k, 1] = send(b, b, ay_s.at[k - 1], ay_r.at[k - 1, 1], ydn)
        give(k, 0)

    def ysecond(k):
        yin[k, 0].wait_recv()
        b = hb.at[k, :, yrel(-1), c, :, pl.ds(0, LH)]
        send(b, b, ay_s.at[k - 1], ay_r.at[k - 1, 2], yup)
        yin[k, 1].wait_recv()
        b = hb.at[k, :, yrel(1), c, :, pl.ds(LH, LH)]
        send(b, b, ay_s.at[k - 1], ay_r.at[k - 1, 2], ydn)
        give(k, 1)
        give(k, 2)

    def ythird(k):
        all_in(hb.at[k, :, yrel(2), c], ay_r.at[k - 1, 2])
        give(k, 3)

    def stage(k, i):
        gives[k, i].wait_recv()
        yb = yrel(GATHER[i])
        ht[...] = hb[k, :, yb].reshape(512, CT).T

        for j in range(NCH):
            cc = pl.ds(j * CW, CW)
            acc = jnp.dot(ht[...], hd[:, yb, :, cc].reshape(512, CW), preferred_element_type=F32)
            if i != 0:
                acc = acc + part[k, :, cc]
            part[k, :, cc] = acc

    def tokens(d, half):
        return pl.ds(pl.multiple_of(xrel(d) * GT + half * GH, GH), GH)

    flying = {}

    def far(k):
        flying[k, 0] = send(part.at[k, tokens(2, 0)], ra1.at[k], rx_s.at[k], rx_r.at[k, 0], xup)
        flying[k, 1] = send(part.at[k, tokens(2, 1)], rb1.at[k], rx_s.at[k], rx_r.at[k, 1], xdn)

    def near(k):
        send(part.at[k, tokens(1, 1)], rr.at[k, 0], rx_s.at[k], rx_r.at[k, 2], xup)
        send(part.at[k, tokens(-1, 0)], rr.at[k, 1], rx_s.at[k], rx_r.at[k, 2], xdn)

    def relay(k):
        flying[k, 0].wait_recv()
        ra1[k] = ra1[k] + part[k, tokens(1, 0), :]
        send(ra1.at[k], rr.at[k, 2], rx_s.at[k], rx_r.at[k, 2], xup)
        flying[k, 1].wait_recv()
        rb1[k] = rb1[k] + part[k, tokens(-1, 1), :]
        send(rb1.at[k], rr.at[k, 3], rx_s.at[k], rx_r.at[k, 2], xdn)

    def final(k):
        all_in(rr.at[k], rx_r.at[k, 2])
        logit[pl.ds(k * GT, GH), :] = part[k, tokens(0, 0), :] + rr[k, 1] + rr[k, 2]
        logit[pl.ds(k * GT + GH, GH), :] = part[k, tokens(0, 1), :] + rr[k, 0] + rr[k, 3]

    def exchange(k, src, dst, ssem, rsem, group):
        for i in FARTHEST:
            send(src, dst.at[k, i], ssem.at[k], rsem.at[k], group(i))

    def local_stats(k):
        @pl.loop(0, GT // 32)
        def _(i):
            r = pl.ds(pl.multiple_of(i * 32, 32), 32)
            t = logit[pl.ds(pl.multiple_of(k * GT + i * 32, 32), 32), :]
            m = jnp.max(t, axis=1, keepdims=True)
            t = t - m
            w = jnp.where(lane == 0, m, wt[k, r, :])
            w = jnp.where(lane == 1, jnp.sum(jnp.exp(t), axis=1, keepdims=True), w)
            for q in range(NT):
                w = jnp.where(lane == 2 + q, jnp.sum(jnp.exp(t * inv[q]), axis=1, keepdims=True), w)
            wt[k, r, :] = w

        flat = wt[k].T
        st[k, 0] = jnp.where(left, flat[0:8, :], pltpu.roll(flat[8:16, :], 64, 1))
        exchange(k, st.at[k, 0], r1, s1_s, s1_r, group1)

    def merge(k, mine, got, rsem):
        all_in(got.at[k, pl.ds(1, 7)], rsem.at[k])
        all_s = [st[k, mine]] + [got[k, i] for i in range(1, 8)]
        top = all_s[0][0:1, :]
        for s in all_s[1:]:
            top = jnp.maximum(top, s[0:1, :])
        acc = None
        for s in all_s:
            t = s * jnp.exp((s[0:1, :] - top) * invc)
            acc = t if acc is None else acc + t
        return top, acc

    def merge1(k):
        top, acc = merge(k, 0, r1, s1_r)
        st[k, 1] = jnp.where(row2 == 0, top, acc)
        exchange(k, st.at[k, 1], r2, s2_s, s2_r, group2)

    base = v * COLS
    col = lax.broadcasted_iota(jnp.int32, (32, CW), 1).astype(F32)

    def grad(k):
        top, acc = merge(k, 1, r2, s2_r)
        acc = jnp.where(wcol > 0.0, acc, 1.0)
        both = jnp.where(row2 == 0, top, wcol / acc)
        ct[pl.ds(0, 8), :] = both
        ct[pl.ds(8, 8), :] = pltpu.roll(both, 64, 1)
        ct[pl.ds(16, 112), :] = jnp.zeros((112, 128), F32)
        coef[...] = ct[...].T

        for p, (j0, j1) in enumerate(PARTS[k]):
            for i in range(GT // 32):
                cf = coef[pl.ds(i * 32, 32), :]
                r = pl.ds(k * GT + i * 32, 32)
                lb = lab[r, 0:1]

                @pl.loop(j0, j1)
                def _(j):
                    cc = pl.ds(pl.multiple_of(j * CW, CW), CW)
                    s = logit[r, cc] - cf[:, 0:1]
                    t = teach[r, cc].astype(F32) - cf[:, 8:9]
                    g = cf[:, 1:2] * jnp.exp(s)
                    g = g - jnp.where(col + (base + j * CW).astype(F32) == lb, mix[0], 0.0)
                    for q in range(NT):
                        g = g + cf[:, 2 + q:3 + q] * jnp.exp(s * inv[q])
                        g = g - cf[:, 9 + q:10 + q] * jnp.exp(t * inv[q])
                    out = pl.ds(pl.multiple_of(k * CT + x * GT + i * 32, 32), 32)
                    grads[out, cc] = g.astype(BF)

            b = gview(k, p, x * GT, GT)
            flying[k, "g", p, 0] = send(b, b, gx_s.at[k], gx_r.at[k, 3 * p], xup)
            flying[k, "g", p, 1] = send(b, b, gx_s.at[k], gx_r.at[k, 3 * p + 1], xdn)

    def gview(k, p, row, rows):
        j0, j1 = PARTS[k][p]
        return grads.at[pl.ds(pl.multiple_of(k * CT + row, GH), rows), pl.ds(j0 * CW, (j1 - j0) * CW)]

    def passon(k, p=0):
        flying[k, "g", p, 0].wait_recv()
        a = gview(k, p, xrel(-1) * GT, GH)
        send(a, a, gx_s.at[k], gx_r.at[k, 3 * p + 2], xup)
        flying[k, "g", p, 1].wait_recv()
        b = gview(k, p, xrel(1) * GT + GH, GH)
        send(b, b, gx_s.at[k], gx_r.at[k, 3 * p + 2], xdn)

    def landed(k):
        for p in range(len(PARTS[k])):
            all_in(gview(k, p, xrel(2) * GT, GT), gx_r.at[k, 3 * p + 2])

    pairs = {}

    def pair(k, i):
        yb = yrel(SPREAD[i])

        def rows_of(cc):
            w = hd[:, yb, pl.ds(pl.multiple_of(cc * LROWS, LROWS), LROWS), :]
            r = lax.dot_general(w.reshape(256, COLS), grads[pl.ds(k * CT, CT), :],
                                (((1,), (1,)), ((), ())), preferred_element_type=F32)
            return r.reshape(NZ, LROWS, CT)

        if (k, i) == (K - 1, 0):
            ps[k, i] = rows_of(1 - c).astype(BF)
        else:
            r = lax.dot_general(hd[:, yb].reshape(512, COLS), grads[pl.ds(k * CT, CT), :],
                                (((1,), (1,)), ((), ())), preferred_element_type=F32)
            tmp[...] = r.reshape(NZ, NC, LROWS, CT)
            ps[k, i] = tmp[:, 1 - c].astype(BF)
        pairs[k, i] = send(ps.at[k, i], pr.at[k, i], pp_s.at[k], pp_r.at[k, i], mate)
        if (k, i) == (K - 1, 0):
            hgo[k, i] = rows_of(c)
        else:
            hgo[k, i] = tmp[:, c]

    LO, HI = pl.ds(0, LH), pl.ds(LH, LH)

    def total(k, i, part_of):
        return hgo[k, i, :, :, part_of] + pr[k, i, :, :, part_of].astype(F32)

    hops = {}

    def yhop(k, i, val, dev):
        ysb[k, i] = val.astype(BF)
        hops[k, i] = send(ysb.at[k, i], yrb.at[k, i], yy_s.at[k], yy_r.at[k, min(i, 2)], dev)

    def scatter(k, step):
        if step == 0:
            pairs[k, 0].wait_recv()
            yhop(k, 0, total(k, 0, LO), yup)
            yhop(k, 1, total(k, 0, HI), ydn)
        elif step == 1:
            pairs[k, 1].wait_recv()
            yhop(k, 2, total(k, 1, HI), yup)
            pairs[k, 2].wait_recv()
            yhop(k, 3, total(k, 2, LO), ydn)
        elif step == 2:
            hops[k, 0].wait_recv()
            yhop(k, 4, total(k, 1, LO) + yrb[k, 0].astype(F32), yup)
            hops[k, 1].wait_recv()
            yhop(k, 5, total(k, 2, HI) + yrb[k, 1].astype(F32), ydn)
        elif step == 3:
            pairs[k, 3].wait_recv()
            all_in(yrb.at[k, pl.ds(2, 4)], yy_r.at[k, 2])
            ysum[:, :, LO] = total(k, 3, LO) + yrb[k, 3].astype(F32) + yrb[k, 4].astype(F32)
            ysum[:, :, HI] = total(k, 3, HI) + yrb[k, 2].astype(F32) + yrb[k, 5].astype(F32)
            zsb[k] = ysum[...].astype(BF)
            res[k] = ysum[z]
            for i in FARTHEST:
                send(zsb.at[k, zrel(i)], zrb.at[k, i], zz_s.at[k], zz_r.at[k], group2(i))
        else:
            all_in(zrb.at[k, pl.ds(1, NZ - 1)], zz_r.at[k])
            acc = res[k]
            for i in range(1, NZ):
                acc = acc + zrb[k, i].astype(F32)
            res[k] = acc

    def head_part(b):
        for j in range(NCH):
            cc = pl.ds(j * CW, CW)
            r = None
            for k in range(K):
                t = jnp.dot(hb[k, b].reshape(256, CT), grads[pl.ds(k * CT, CT), cc],
                            preferred_element_type=F32)
                r = t if r is None else r + t
            hdgrad[pl.ds(b * 256, 256), cc] = r.astype(BF)

    NEAREST = (1, 7, 2, 6, 3, 5, 4)
    for i in NEAREST:
        zin[0, i].wait_recv()
        piece_out(i)
        if i == 7:
            zsend(1)
    give(0, 0)
    zsend(2)
    for i in (0,) + NEAREST:
        piece_on(i)
    give(0, 1)
    give(0, 2)
    head_copy.wait()
    stage(0, 0)
    yfirst(1)
    stage(0, 1)
    stage(0, 2)
    far_y = hb.at[0, :, yrel(2), c]
    all_in(far_y.at[:, :, pl.ds(0, LH)], fq_r.at[0])
    all_in(far_y.at[:, :, pl.ds(LH, LH)], fq_r.at[1])
    give(0, 3)
    stage(0, 3)
    far(0)
    near(0)
    ysecond(1)
    teacher_stats(1)
    stage(1, 0)
    yfirst(2)
    stage(1, 1)
    stage(1, 2)
    relay(0)
    ythird(1)
    stage(1, 3)
    far(1)
    near(1)
    teacher_stats(2)
    ysecond(2)
    stage(2, 0)
    stage(2, 1)
    stage(2, 2)
    ythird(2)
    final(0)
    local_stats(0)
    stage(2, 3)
    far(2)
    relay(1)
    near(2)
    merge1(0)
    relay(2)
    grad(0)
    final(1)
    local_stats(1)
    merge1(1)
    final(2)
    local_stats(2)
    passon(0)
    grad(1)
    merge1(2)
    landed(0)
    pair(0, 0)
    pair(0, 1)
    scatter(0, 0)
    passon(1)
    grad(2)
    pair(0, 2)
    pair(0, 3)
    scatter(0, 1)
    scatter(0, 2)
    landed(1)
    pair(1, 0)
    pair(1, 1)
    scatter(1, 0)
    passon(2, 0)
    pair(1, 2)
    passon(2, 1)
    pair(1, 3)
    scatter(1, 1)
    landed(2)
    pair(2, 0)
    scatter(1, 2)
    pair(2, 1)
    scatter(2, 0)
    scatter(0, 3)
    pair(2, 2)
    pair(2, 3)
    scatter(2, 1)
    head_part(0)
    head_part(1)
    head_part(2)
    scatter(2, 2)
    scatter(1, 3)
    head_part(3)
    head_part(4)
    head_part(5)
    scatter(2, 3)
    for b in (6, 7):
        head_part(b)
    scatter(0, 4)
    scatter(1, 4)
    scatter(2, 4)

    full = [res[k] for k in range(K)]
    hgrad[...] = jnp.concatenate(
        [full[k][:, d * GT:(d + 1) * GT] for d in range(NX) for k in range(K)], axis=1)

    one = hb.at[0, :, y, c]
    for i in (0, 1):
        all_out(one, fy_s.at[i])
        all_out(one.at[:, :, pl.ds(0, LH)], fy_s.at[2 + i])
    for k in range(K):
        all_out(hb.at[k, pl.ds(0, NZ - 1), y, c], az_s.at[k])
        all_out(hb.at[k, :, :, c], ap_s.at[k])
        if k > 0:
            all_out(hb.at[k, :, pl.ds(0, 3), c], ay_s.at[k - 1])
        all_out(logit, rx_s.at[k])
        all_out(r1.at[k, pl.ds(1, 7)], s1_s.at[k])
        all_out(r2.at[k, pl.ds(1, 7)], s2_s.at[k])
        all_out(grads.at[pl.ds(0, OWN)], gx_s.at[k])
        all_out(ps.at[k], pp_s.at[k])
        all_out(ysb.at[k], yy_s.at[k])
        all_out(zrb.at[k, pl.ds(1, NZ - 1)], zz_s.at[k])


def shards(hidden_t, head, teacher, labels, temps, mix):
    vmem = pl.BlockSpec(memory_space=pltpu.VMEM)
    hbm = pl.BlockSpec(memory_space=pl.ANY)
    dma = pltpu.SemaphoreType.DMA
    half = (K, GH, COLS)
    return pl.pallas_call(
        body,
        out_shape=(
            pltpu.VMEM((LROWS, TOK), F32),
            pltpu.VMEM((FEAT, COLS), BF),
        ),
        in_specs=[hbm] * 6,
        out_specs=(vmem, vmem),
        scratch_shapes=[
            pltpu.VMEM((LROWS, TOK), BF),
            pltpu.VMEM((1, OWN), jnp.int32),
            pltpu.SMEM((NT,), F32),
            pltpu.SMEM((2,), F32),
            pltpu.VMEM((K, NZ, NY, NC, LROWS, CT), BF),
            pltpu.VMEM((NZ, NY, NC * LROWS, COLS), BF),
            pltpu.VMEM((CT, 512), BF),
            pltpu.VMEM((K, CT, COLS), F32),
            pltpu.VMEM(half, F32), pltpu.VMEM(half, F32),
            pltpu.VMEM((K, 4, GH, COLS), F32),
            pltpu.VMEM((OWN, COLS), F32),
            pltpu.VMEM((OWN, COLS), BF),
            pltpu.VMEM((K, 128, 128), F32),
            pltpu.VMEM((K, 2, 8, 128), F32),
            pltpu.VMEM((K, 8, 8, 128), F32),
            pltpu.VMEM((K, 8, 8, 128), F32),
            pltpu.VMEM((128, 128), F32),
            pltpu.VMEM((128, 128), F32),
            pltpu.VMEM((256, 128), F32),
            pltpu.VMEM((TOK, COLS), BF),
            pltpu.VMEM((NZ, NC, LROWS, CT), F32),
            pltpu.VMEM((K, NY, NZ, LROWS, CT), F32),
            pltpu.VMEM((K, NY, NZ, LROWS, CT), BF),
            pltpu.VMEM((K, NY, NZ, LROWS, CT), BF),
            pltpu.VMEM((K, 6, NZ, LROWS, LH), BF),
            pltpu.VMEM((K, 6, NZ, LROWS, LH), BF),
            pltpu.VMEM((NZ, LROWS, CT), F32),
            pltpu.VMEM((K, NZ, LROWS, CT), BF),
            pltpu.VMEM((K, NZ, LROWS, CT), BF),
            pltpu.VMEM((K, LROWS, CT), F32),
            dma((6,)),
            dma((4,)), dma((NZ, 2)), dma((2,)),
            dma((K - 1,)), dma((K - 1, 3)),
            dma((K,)), dma((6 + K,)),
            dma((K,)), dma((K, 4)),
            dma((K,)), dma((K, 3)),
            dma((K,)), dma((K,)),
            dma((K,)), dma((K,)),
            dma((K,)), dma((K, 6)),
            dma((K,)), dma((K, 4)),
            dma((K,)), dma((K,)),
            dma((K,)), dma((K, 3)),
        ],
        compiler_params=pltpu.CompilerParams(
            collective_id=0, has_side_effects=True, vmem_limit_bytes=56 * 1024 * 1024
        ),
    )(hidden_t, head.reshape(NZ, NY, NC * LROWS, COLS), teacher, labels.reshape(1, OWN), temps, mix)


def solution(mesh):
    placed = (P(("dp", "vocab"), None), P("dp", "vocab"), P("dp", "vocab"), P("dp"), P(), P())
    return jax.shard_map(
        shards,
        mesh=mesh,
        in_specs=placed,
        out_specs=(P(("dp", "vocab"), None), P("dp", "vocab")),
        check_vma=False,
    )
```

```python
import jax
import jax.numpy as jnp
from jax import lax
from jax.experimental import pallas as pl
from jax.experimental.pallas import tpu as pltpu
from jax.sharding import PartitionSpec as P

BF = jnp.bfloat16
F32 = jnp.float32
MESH = pl.DeviceIdType.MESH
NX, NZ, NY, NC = 4, 8, 4, 2
TOK, OWN = 768, 192
K = 3
CT = TOK // K
GT = CT // NX
GH = GT // 2
LH = CT // 2
COLS, CW, NCH = 1280, 256, 5
FEAT, LROWS = 2048, 32
NT = 4
GATHER = (0, -1, 1, 2)
SPREAD = (2, 1, -1, 0)
FARTHEST = (4, 3, 5, 2, 6, 1, 7)
PARTS = (((0, 5),), ((0, 3), (3, 5)), ((0, 3), (3, 5)))


def body(hid_hbm, head_hbm, teach_hbm, labels_hbm, temps_hbm, mix_hbm,
         hgrad, hdgrad,
         hid, labels, temps, mix,
         hb, hd, ht, part, ra1, rb1, rr, logit, teach,
         wt, st, r1, r2, ct, coef, lab, grads, tmp, hgo, ps, pr, ysb, yrb, ysum, zsb, zrb, res,
         loc_sem, fy_s, fy_r, fq_r, ay_s, ay_r, az_s, az_r, ap_s, ap_r,
         rx_s, rx_r, s1_s, s1_r, s2_s, s2_r, gx_s, gx_r,
         pp_s, pp_r, zz_s, zz_r, yy_s, yy_r):
    x = lax.axis_index("dp")
    v = lax.axis_index("vocab")
    c = lax.rem(v, 2)
    y = lax.rem(v // 2, NY)
    z = v // (NY * NC)

    def vid(zz, yy, cc):
        return {"vocab": (zz * NY + yy) * NC + cc}

    def zrel(d):
        return lax.rem(z + (d + NZ), NZ)

    def yrel(d):
        return lax.rem(y + (d + NY), NY)

    def xrel(d):
        return lax.rem(x + (d + NX), NX)

    yup, ydn = vid(z, yrel(1), c), vid(z, yrel(-1), c)
    mate = vid(z, y, 1 - c)
    xup, xdn = {"dp": xrel(1)}, {"dp": xrel(-1)}
    slot = y * NC + c

    def group1(k):
        other = lax.rem(slot + k, 8)
        return vid(z, other // NC, lax.rem(other, NC))

    def group2(k):
        return vid(zrel(k), y, c)

    def send(src, dst, ssem, rsem, dev):
        cp = pltpu.make_async_remote_copy(
            src_ref=src, dst_ref=dst, send_sem=ssem, recv_sem=rsem,
            device_id=dev, device_id_type=MESH)
        cp.start()
        return cp

    def all_in(ref, sem):
        pltpu.make_async_remote_copy(
            src_ref=ref, dst_ref=ref, send_sem=sem, recv_sem=sem,
            device_id=mate, device_id_type=MESH).wait_recv()

    def all_out(ref, sem):
        pltpu.make_async_remote_copy(
            src_ref=ref, dst_ref=ref, send_sem=sem, recv_sem=sem,
            device_id=mate, device_id_type=MESH).wait_send()

    small = []
    for n, (a, b) in enumerate(((hid_hbm, hid), (labels_hbm, labels), (temps_hbm, temps), (mix_hbm, mix))):
        cp = pltpu.make_async_copy(a, b, loc_sem.at[2 + n])
        cp.start()
        small.append(cp)

    bar = pltpu.get_barrier_semaphore()
    for k in range(4, 0, -1):
        for i in {4: (4,)}.get(k, (k, NZ - k)):
            pl.semaphore_signal(bar, inc=1, device_id=group2(i), device_id_type=MESH)
    for k in range(1, 8):
        pl.semaphore_signal(bar, inc=1, device_id=group1(k), device_id_type=MESH)
    pl.semaphore_signal(bar, inc=1, device_id=xup, device_id_type=MESH)
    pl.semaphore_signal(bar, inc=1, device_id=xdn, device_id_type=MESH)

    head_copy = pltpu.make_async_copy(head_hbm, hd, loc_sem.at[0])
    head_copy.start()
    teach_copy = pltpu.make_async_copy(teach_hbm, teach, loc_sem.at[1])
    teach_copy.start()

    for cp in small:
        cp.wait()

    h32 = hid[...].astype(F32)
    for k in range(K):
        piece = jnp.concatenate(
            [h32[:, d * OWN + k * GT:d * OWN + (k + 1) * GT] for d in range(NX)], axis=1)
        hb[k, z, y, c] = piece.astype(BF)

    pl.semaphore_wait(bar, 16)

    zin = {}
    fin = {}

    def zsend(k):
        own = hb.at[k, z, y, c]
        for i in FARTHEST:
            zin[k, i] = send(own, own, az_s.at[k], az_r.at[i - 1 if k == 0 else 6 + k], group2(i))

    def piece_out(i):
        b = hb.at[0, zrel(-i), y, c]
        fin[i, 0] = send(b, b, fy_s.at[0], fy_r.at[i, 0], yup)
        fin[i, 1] = send(b, b, fy_s.at[1], fy_r.at[i, 1], ydn)

    def piece_on(i):
        fin[i, 0].wait_recv()
        b = hb.at[0, zrel(-i), yrel(-1), c, :, pl.ds(0, LH)]
        send(b, b, fy_s.at[2], fq_r.at[0], yup)
        fin[i, 1].wait_recv()
        b = hb.at[0, zrel(-i), yrel(1), c, :, pl.ds(LH, LH)]
        send(b, b, fy_s.at[3], fq_r.at[1], ydn)

    zsend(0)
    piece_out(0)

    inv = [1.0 / temps[q] for q in range(NT)]
    lane = lax.broadcasted_iota(jnp.int32, (32, 128), 1)
    row2 = lax.broadcasted_iota(jnp.int32, (8, 128), 0)
    left = lax.broadcasted_iota(jnp.int32, (8, 128), 1) < 64
    invc = jnp.where(left & (row2 == 1), 1.0, 0.0)
    wcol = jnp.where(left & (row2 == 1), mix[0], 0.0)
    for q in range(NT):
        hit = (left & (row2 == 2 + q)) | (jnp.logical_not(left) & (row2 == 1 + q))
        invc = jnp.where(hit, inv[q], invc)
        wcol = jnp.where(hit, mix[1] * temps[q], wcol)

    lab[...] = jnp.zeros((256, 128), F32)
    labrow = jnp.concatenate(
        [labels[...].astype(F32), jnp.zeros((1, 256 - OWN), F32)], axis=1)
    lab[...] = jnp.broadcast_to(labrow, (128, 256)).T

    teach_copy.wait()

    def teacher_stats(k):
        @pl.loop(0, GT // 32)
        def _(i):
            r = pl.ds(pl.multiple_of(i * 32, 32), 32)
            t = teach[pl.ds(pl.multiple_of(k * GT + i * 32, 32), 32), :].astype(F32)
            m = jnp.max(t, axis=1, keepdims=True)
            t = t - m
            w = jnp.where(lane == 8, m, 0.0)
            for q in range(NT):
                w = jnp.where(lane == 9 + q, jnp.sum(jnp.exp(t * inv[q]), axis=1, keepdims=True), w)
            wt[k, r, :] = w

        wt[k, pl.ds(GT, 128 - GT), :] = jnp.zeros((128 - GT, 128), F32)

    teacher_stats(0)

    yin = {}
    gives = {}

    def bundle(k, d):
        return hb.at[k, :, yrel(d), c]

    def give(k, i):
        b = bundle(k, GATHER[i])
        gives[k, i] = send(b, b, ap_s.at[k], ap_r.at[k, i], mate)

    def yfirst(k):
        all_in(hb.at[k, pl.ds(0, NZ - 1), y, c], az_r.at[6 + k])
        b = bundle(k, 0)
        yin[k, 0] = send(b, b, ay_s.at[k - 1], ay_r.at[k - 1, 0], yup)
        yin[k, 1] = send(b, b, ay_s.at[k - 1], ay_r.at[k - 1, 1], ydn)
        give(k, 0)

    def ysecond(k):
        yin[k, 0].wait_recv()
        b = hb.at[k, :, yrel(-1), c, :, pl.ds(0, LH)]
        send(b, b, ay_s.at[k - 1], ay_r.at[k - 1, 2], yup)
        yin[k, 1].wait_recv()
        b = hb.at[k, :, yrel(1), c, :, pl.ds(LH, LH)]
        send(b, b, ay_s.at[k - 1], ay_r.at[k - 1, 2], ydn)
        give(k, 1)
        give(k, 2)

    def ythird(k):
        all_in(hb.at[k, :, yrel(2), c], ay_r.at[k - 1, 2])
        give(k, 3)

    def stage(k, i):
        gives[k, i].wait_recv()
        yb = yrel(GATHER[i])
        ht[...] = hb[k, :, yb].reshape(512, CT).T

        for j in range(NCH):
            cc = pl.ds(j * CW, CW)
            acc = jnp.dot(ht[...], hd[:, yb, :, cc].reshape(512, CW), preferred_element_type=F32)
            if i != 0:
                acc = acc + part[k, :, cc]
            part[k, :, cc] = acc

    def tokens(d, half):
        return pl.ds(pl.multiple_of(xrel(d) * GT + half * GH, GH), GH)

    flying = {}

    def far(k):
        flying[k, 0] = send(part.at[k, tokens(2, 0)], ra1.at[k], rx_s.at[k], rx_r.at[k, 0], xup)
        flying[k, 1] = send(part.at[k, tokens(2, 1)], rb1.at[k], rx_s.at[k], rx_r.at[k, 1], xdn)

    def near(k):
        send(part.at[k, tokens(1, 1)], rr.at[k, 0], rx_s.at[k], rx_r.at[k, 2], xup)
        send(part.at[k, tokens(-1, 0)], rr.at[k, 1], rx_s.at[k], rx_r.at[k, 2], xdn)

    def relay(k):
        flying[k, 0].wait_recv()
        ra1[k] = ra1[k] + part[k, tokens(1, 0), :]
        send(ra1.at[k], rr.at[k, 2], rx_s.at[k], rx_r.at[k, 2], xup)
        flying[k, 1].wait_recv()
        rb1[k] = rb1[k] + part[k, tokens(-1, 1), :]
        send(rb1.at[k], rr.at[k, 3], rx_s.at[k], rx_r.at[k, 2], xdn)

    def final(k):
        all_in(rr.at[k], rx_r.at[k, 2])
        logit[pl.ds(k * GT, GH), :] = part[k, tokens(0, 0), :] + rr[k, 1] + rr[k, 2]
        logit[pl.ds(k * GT + GH, GH), :] = part[k, tokens(0, 1), :] + rr[k, 0] + rr[k, 3]

    def exchange(k, src, dst, ssem, rsem, group):
        for i in FARTHEST:
            send(src, dst.at[k, i], ssem.at[k], rsem.at[k], group(i))

    def local_stats(k):
        @pl.loop(0, GT // 32)
        def _(i):
            r = pl.ds(pl.multiple_of(i * 32, 32), 32)
            t = logit[pl.ds(pl.multiple_of(k * GT + i * 32, 32), 32), :]
            m = jnp.max(t, axis=1, keepdims=True)
            t = t - m
            w = jnp.where(lane == 0, m, wt[k, r, :])
            w = jnp.where(lane == 1, jnp.sum(jnp.exp(t), axis=1, keepdims=True), w)
            for q in range(NT):
                w = jnp.where(lane == 2 + q, jnp.sum(jnp.exp(t * inv[q]), axis=1, keepdims=True), w)
            wt[k, r, :] = w

        flat = wt[k].T
        st[k, 0] = jnp.where(left, flat[0:8, :], pltpu.roll(flat[8:16, :], 64, 1))
        exchange(k, st.at[k, 0], r1, s1_s, s1_r, group1)

    def merge(k, mine, got, rsem):
        all_in(got.at[k, pl.ds(1, 7)], rsem.at[k])
        all_s = [st[k, mine]] + [got[k, i] for i in range(1, 8)]
        top = all_s[0][0:1, :]
        for s in all_s[1:]:
            top = jnp.maximum(top, s[0:1, :])
        acc = None
        for s in all_s:
            t = s * jnp.exp((s[0:1, :] - top) * invc)
            acc = t if acc is None else acc + t
        return top, acc

    def merge1(k):
        top, acc = merge(k, 0, r1, s1_r)
        st[k, 1] = jnp.where(row2 == 0, top, acc)
        exchange(k, st.at[k, 1], r2, s2_s, s2_r, group2)

    base = v * COLS
    col = lax.broadcasted_iota(jnp.int32, (32, CW), 1).astype(F32)

    def grad(k):
        top, acc = merge(k, 1, r2, s2_r)
        acc = jnp.where(wcol > 0.0, acc, 1.0)
        both = jnp.where(row2 == 0, top, wcol / acc)
        ct[pl.ds(0, 8), :] = both
        ct[pl.ds(8, 8), :] = pltpu.roll(both, 64, 1)
        ct[pl.ds(16, 112), :] = jnp.zeros((112, 128), F32)
        coef[...] = ct[...].T

        for p, (j0, j1) in enumerate(PARTS[k]):
            for i in range(GT // 32):
                cf = coef[pl.ds(i * 32, 32), :]
                r = pl.ds(k * GT + i * 32, 32)
                lb = lab[r, 0:1]

                @pl.loop(j0, j1)
                def _(j):
                    cc = pl.ds(pl.multiple_of(j * CW, CW), CW)
                    s = logit[r, cc] - cf[:, 0:1]
                    t = teach[r, cc].astype(F32) - cf[:, 8:9]
                    g = cf[:, 1:2] * jnp.exp(s)
                    g = g - jnp.where(col + (base + j * CW).astype(F32) == lb, mix[0], 0.0)
                    for q in range(NT):
                        g = g + cf[:, 2 + q:3 + q] * jnp.exp(s * inv[q])
                        g = g - cf[:, 9 + q:10 + q] * jnp.exp(t * inv[q])
                    out = pl.ds(pl.multiple_of(k * CT + x * GT + i * 32, 32), 32)
                    grads[out, cc] = g.astype(BF)

            b = gview(k, p, x * GT, GT)
            flying[k, "g", p, 0] = send(b, b, gx_s.at[k], gx_r.at[k, 3 * p], xup)
            flying[k, "g", p, 1] = send(b, b, gx_s.at[k], gx_r.at[k, 3 * p + 1], xdn)

    def gview(k, p, row, rows):
        j0, j1 = PARTS[k][p]
        return grads.at[pl.ds(pl.multiple_of(k * CT + row, GH), rows), pl.ds(j0 * CW, (j1 - j0) * CW)]

    def passon(k, p=0):
        flying[k, "g", p, 0].wait_recv()
        a = gview(k, p, xrel(-1) * GT, GH)
        send(a, a, gx_s.at[k], gx_r.at[k, 3 * p + 2], xup)
        flying[k, "g", p, 1].wait_recv()
        b = gview(k, p, xrel(1) * GT + GH, GH)
        send(b, b, gx_s.at[k], gx_r.at[k, 3 * p + 2], xdn)

    def landed(k):
        for p in range(len(PARTS[k])):
            all_in(gview(k, p, xrel(2) * GT, GT), gx_r.at[k, 3 * p + 2])

    pairs = {}

    def pair(k, i):
        yb = yrel(SPREAD[i])

        def rows_of(cc):
            w = hd[:, yb, pl.ds(pl.multiple_of(cc * LROWS, LROWS), LROWS), :]
            r = lax.dot_general(w.reshape(256, COLS), grads[pl.ds(k * CT, CT), :],
                                (((1,), (1,)), ((), ())), preferred_element_type=F32)
            return r.reshape(NZ, LROWS, CT)

        if (k, i) == (K - 1, 0):
            ps[k, i] = rows_of(1 - c).astype(BF)
        else:
            r = lax.dot_general(hd[:, yb].reshape(512, COLS), grads[pl.ds(k * CT, CT), :],
                                (((1,), (1,)), ((), ())), preferred_element_type=F32)
            tmp[...] = r.reshape(NZ, NC, LROWS, CT)
            ps[k, i] = tmp[:, 1 - c].astype(BF)
        pairs[k, i] = send(ps.at[k, i], pr.at[k, i], pp_s.at[k], pp_r.at[k, i], mate)
        if (k, i) == (K - 1, 0):
            hgo[k, i] = rows_of(c)
        else:
            hgo[k, i] = tmp[:, c]

    LO, HI = pl.ds(0, LH), pl.ds(LH, LH)

    def total(k, i, part_of):
        return hgo[k, i, :, :, part_of] + pr[k, i, :, :, part_of].astype(F32)

    hops = {}

    def yhop(k, i, val, dev):
        ysb[k, i] = val.astype(BF)
        hops[k, i] = send(ysb.at[k, i], yrb.at[k, i], yy_s.at[k], yy_r.at[k, min(i, 2)], dev)

    def scatter(k, step):
        if step == 0:
            pairs[k, 0].wait_recv()
            yhop(k, 0, total(k, 0, LO), yup)
            yhop(k, 1, total(k, 0, HI), ydn)
        elif step == 1:
            pairs[k, 1].wait_recv()
            yhop(k, 2, total(k, 1, HI), yup)
            pairs[k, 2].wait_recv()
            yhop(k, 3, total(k, 2, LO), ydn)
        elif step == 2:
            hops[k, 0].wait_recv()
            yhop(k, 4, total(k, 1, LO) + yrb[k, 0].astype(F32), yup)
            hops[k, 1].wait_recv()
            yhop(k, 5, total(k, 2, HI) + yrb[k, 1].astype(F32), ydn)
        elif step == 3:
            pairs[k, 3].wait_recv()
            all_in(yrb.at[k, pl.ds(2, 4)], yy_r.at[k, 2])
            ysum[:, :, LO] = total(k, 3, LO) + yrb[k, 3].astype(F32) + yrb[k, 4].astype(F32)
            ysum[:, :, HI] = total(k, 3, HI) + yrb[k, 2].astype(F32) + yrb[k, 5].astype(F32)
            zsb[k] = ysum[...].astype(BF)
            res[k] = ysum[z]
            for i in FARTHEST:
                send(zsb.at[k, zrel(i)], zrb.at[k, i], zz_s.at[k], zz_r.at[k], group2(i))
        else:
            all_in(zrb.at[k, pl.ds(1, NZ - 1)], zz_r.at[k])
            acc = res[k]
            for i in range(1, NZ):
                acc = acc + zrb[k, i].astype(F32)
            res[k] = acc

    def head_part(b):
        for j in range(NCH):
            cc = pl.ds(j * CW, CW)
            r = None
            for k in range(K):
                t = jnp.dot(hb[k, b].reshape(256, CT), grads[pl.ds(k * CT, CT), cc],
                            preferred_element_type=F32)
                r = t if r is None else r + t
            hdgrad[pl.ds(b * 256, 256), cc] = r.astype(BF)

    NEAREST = (1, 7, 2, 6, 3, 5, 4)
    for i in NEAREST:
        zin[0, i].wait_recv()
        piece_out(i)
        if i == 7:
            zsend(1)
    give(0, 0)
    zsend(2)
    for i in (0,) + NEAREST:
        piece_on(i)
    give(0, 1)
    give(0, 2)
    head_copy.wait()
    stage(0, 0)
    yfirst(1)
    stage(0, 1)
    stage(0, 2)
    far_y = hb.at[0, :, yrel(2), c]
    all_in(far_y.at[:, :, pl.ds(0, LH)], fq_r.at[0])
    all_in(far_y.at[:, :, pl.ds(LH, LH)], fq_r.at[1])
    give(0, 3)
    stage(0, 3)
    far(0)
    near(0)
    ysecond(1)
    teacher_stats(1)
    stage(1, 0)
    yfirst(2)
    stage(1, 1)
    stage(1, 2)
    relay(0)
    ythird(1)
    stage(1, 3)
    far(1)
    near(1)
    teacher_stats(2)
    ysecond(2)
    stage(2, 0)
    stage(2, 1)
    stage(2, 2)
    ythird(2)
    final(0)
    local_stats(0)
    stage(2, 3)
    far(2)
    relay(1)
    near(2)
    merge1(0)
    relay(2)
    grad(0)
    final(1)
    local_stats(1)
    merge1(1)
    final(2)
    local_stats(2)
    passon(0)
    grad(1)
    merge1(2)
    landed(0)
    pair(0, 0)
    pair(0, 1)
    scatter(0, 0)
    passon(1, 0)
    grad(2)
    passon(1, 1)
    pair(0, 2)
    pair(0, 3)
    scatter(0, 1)
    scatter(0, 2)
    landed(1)
    pair(1, 0)
    pair(1, 1)
    scatter(1, 0)
    passon(2, 0)
    pair(1, 2)
    passon(2, 1)
    pair(1, 3)
    scatter(1, 1)
    landed(2)
    pair(2, 0)
    scatter(1, 2)
    pair(2, 1)
    scatter(2, 0)
    scatter(0, 3)
    pair(2, 2)
    pair(2, 3)
    scatter(2, 1)
    head_part(0)
    head_part(1)
    head_part(2)
    scatter(2, 2)
    scatter(1, 3)
    head_part(3)
    head_part(4)
    head_part(5)
    scatter(2, 3)
    for b in (6, 7):
        head_part(b)
    scatter(0, 4)
    scatter(1, 4)
    scatter(2, 4)

    full = [res[k] for k in range(K)]
    hgrad[...] = jnp.concatenate(
        [full[k][:, d * GT:(d + 1) * GT] for d in range(NX) for k in range(K)], axis=1)

    one = hb.at[0, :, y, c]
    for i in (0, 1):
        all_out(one, fy_s.at[i])
        all_out(one.at[:, :, pl.ds(0, LH)], fy_s.at[2 + i])
    for k in range(K):
        all_out(hb.at[k, pl.ds(0, NZ - 1), y, c], az_s.at[k])
        all_out(hb.at[k, :, :, c], ap_s.at[k])
        if k > 0:
            all_out(hb.at[k, :, pl.ds(0, 3), c], ay_s.at[k - 1])
        all_out(logit, rx_s.at[k])
        all_out(r1.at[k, pl.ds(1, 7)], s1_s.at[k])
        all_out(r2.at[k, pl.ds(1, 7)], s2_s.at[k])
        all_out(grads.at[pl.ds(0, OWN)], gx_s.at[k])
        all_out(ps.at[k], pp_s.at[k])
        all_out(ysb.at[k], yy_s.at[k])
        all_out(zrb.at[k, pl.ds(1, NZ - 1)], zz_s.at[k])


def shards(hidden_t, head, teacher, labels, temps, mix):
    vmem = pl.BlockSpec(memory_space=pltpu.VMEM)
    hbm = pl.BlockSpec(memory_space=pl.ANY)
    dma = pltpu.SemaphoreType.DMA
    half = (K, GH, COLS)
    return pl.pallas_call(
        body,
        out_shape=(
            pltpu.VMEM((LROWS, TOK), F32),
            pltpu.VMEM((FEAT, COLS), BF),
        ),
        in_specs=[hbm] * 6,
        out_specs=(vmem, vmem),
        scratch_shapes=[
            pltpu.VMEM((LROWS, TOK), BF),
            pltpu.VMEM((1, OWN), jnp.int32),
            pltpu.SMEM((NT,), F32),
            pltpu.SMEM((2,), F32),
            pltpu.VMEM((K, NZ, NY, NC, LROWS, CT), BF),
            pltpu.VMEM((NZ, NY, NC * LROWS, COLS), BF),
            pltpu.VMEM((CT, 512), BF),
            pltpu.VMEM((K, CT, COLS), F32),
            pltpu.VMEM(half, F32), pltpu.VMEM(half, F32),
            pltpu.VMEM((K, 4, GH, COLS), F32),
            pltpu.VMEM((OWN, COLS), F32),
            pltpu.VMEM((OWN, COLS), BF),
            pltpu.VMEM((K, 128, 128), F32),
            pltpu.VMEM((K, 2, 8, 128), F32),
            pltpu.VMEM((K, 8, 8, 128), F32),
            pltpu.VMEM((K, 8, 8, 128), F32),
            pltpu.VMEM((128, 128), F32),
            pltpu.VMEM((128, 128), F32),
            pltpu.VMEM((256, 128), F32),
            pltpu.VMEM((TOK, COLS), BF),
            pltpu.VMEM((NZ, NC, LROWS, CT), F32),
            pltpu.VMEM((K, NY, NZ, LROWS, CT), F32),
            pltpu.VMEM((K, NY, NZ, LROWS, CT), BF),
            pltpu.VMEM((K, NY, NZ, LROWS, CT), BF),
            pltpu.VMEM((K, 6, NZ, LROWS, LH), BF),
            pltpu.VMEM((K, 6, NZ, LROWS, LH), BF),
            pltpu.VMEM((NZ, LROWS, CT), F32),
            pltpu.VMEM((K, NZ, LROWS, CT), BF),
            pltpu.VMEM((K, NZ, LROWS, CT), BF),
            pltpu.VMEM((K, LROWS, CT), F32),
            dma((6,)),
            dma((4,)), dma((NZ, 2)), dma((2,)),
            dma((K - 1,)), dma((K - 1, 3)),
            dma((K,)), dma((6 + K,)),
            dma((K,)), dma((K, 4)),
            dma((K,)), dma((K, 3)),
            dma((K,)), dma((K,)),
            dma((K,)), dma((K,)),
            dma((K,)), dma((K, 6)),
            dma((K,)), dma((K, 4)),
            dma((K,)), dma((K,)),
            dma((K,)), dma((K, 3)),
        ],
        compiler_params=pltpu.CompilerParams(
            collective_id=0, has_side_effects=True, vmem_limit_bytes=56 * 1024 * 1024
        ),
    )(hidden_t, head.reshape(NZ, NY, NC * LROWS, COLS), teacher, labels.reshape(1, OWN), temps, mix)


def solution(mesh):
    placed = (P(("dp", "vocab"), None), P("dp", "vocab"), P("dp", "vocab"), P("dp"), P(), P())
    return jax.shard_map(
        shards,
        mesh=mesh,
        in_specs=placed,
        out_specs=(P(("dp", "vocab"), None), P("dp", "vocab")),
        check_vma=False,
    )
```
